256 devices in a mesh: rows: 16 (over z_hi, y, core), cols: 16 (over z_lo, x).
Axes of the slice: x: 4, y: 4, z: 8 (z_hi: 2, z_lo: 4; z = z_hi * 4 + z_lo), core: 2. Of those that a mesh axis runs over, the one named last changes fastest.
Arguments:
- single: bfloat16 [2048, 1024], P('rows'), may hold values from -6 to 6
- pair: bfloat16 [2048, 2048, 128], P('rows', 'cols'), may hold values from -6 to 6
- residue_mask: int32 [2048], replicated, may hold values from 0 to 1, as said below
- w_bias: bfloat16 [128, 32], replicated, may hold values from -40 to 40
- w_project: bfloat16 [4, 1024, 1024], P(None, None, 'cols'), may hold values from -0.1875 to 0.1875
- w_out: bfloat16 [1024, 1024], replicated, may hold values from -0.1875 to 0.1875
- w_factors: bfloat16 [1024, 128], replicated, may hold values from -0.1875 to 0.1875
- w_pairout: bfloat16 [128, 128], replicated, may hold values from -0.5 to 0.5
- w_up: bfloat16 [128, 512], replicated, may hold values from -0.5 to 0.5
- w_down: bfloat16 [512, 128], replicated, may hold values from -0.25 to 0.25
Outputs:
- single_out: bfloat16 [2048, 1024], P('rows')
- pair_out: bfloat16 [2048, 2048, 128], P('rows', 'cols')
The draws below stay inside these ranges and needn't reach their ends.
Inputs may be any that keep to these rules, and one draw needn't show every extreme that they name: residue_mask is 1 on a leading run of at least 1024 positions and 0 after it.
All inputs are finite; a program needn't handle non-finite values.
Results may differ from the reference program's by a relative error of at most 0.01.
The reference program's roundings to bfloat16 on the way count: a program that leaves them out, or rounds other values in their place, can miss the bound.
Values may be sent and summed in bfloat16 or wider, within the bound.
No kernel may reach another device: no remote copies, remote signals or barrier semaphores. Data moves between devices by JAX's collectives and lax.ppermute only.
A program may use at most 64 MiB of HBM per device.

```python
import math
import jax
import jax.numpy as jnp
from jax import lax

SINGLE = 1024
HEADS = 32
HEAD_DIM = 32
PAIR = 128
PAIR_HID = 512
OPD = 64
RESIDUES = 2048


def draw_residue_mask(key, part):
    length_now = jax.random.randint(jax.random.fold_in(key, 11), (), RESIDUES // 2, RESIDUES + 1)
    return (jnp.arange(RESIDUES, dtype=jnp.int32) < length_now).astype(jnp.int32)


def draw_w_bias(key, part):
    drawn = jax.random.normal(jax.random.fold_in(key, 23), (PAIR, HEADS), jnp.float32) / jnp.sqrt(jnp.float32(PAIR))
    return jnp.clip(drawn, -40.0, 40.0).astype(jnp.bfloat16)


def block_levels(key, shape, split, smallest, high):
    gain, own = 1.0, jax.random.fold_in(key, 6)
    for position, blocks in split:
        steps = jnp.exp(jax.random.uniform(jax.random.fold_in(own, position), (blocks,), jnp.float32, smallest / len(split), high / len(split)))
        gain = gain * jnp.repeat(steps, shape[position] // blocks).reshape([-1 if axis == position else 1 for axis in range(len(shape))])
    return gain


def scatter_about(stream_key, dims, deviation, limit, split=(), kind=jnp.bfloat16):
    entries = deviation * jax.random.normal(stream_key, dims, jnp.float32)
    if split:
        entries = entries * block_levels(stream_key, dims, split, -0.22, 0.18)
    return jnp.clip(entries, -limit, limit).astype(kind)


def setup_inputs(seed: int = 0) -> dict:
    streams_of = jax.random.split(jax.random.key(seed), 11)
    return {
        "single": scatter_about(streams_of[0], (RESIDUES, SINGLE), 1.0, 6.0, ((0, 16),)),
        "pair": scatter_about(streams_of[1], (RESIDUES, RESIDUES, PAIR), 1.0, 6.0, ((0, 16), (1, 16))),
        "residue_mask": draw_residue_mask(jax.random.fold_in(streams_of[10], 71), 0),
        "w_bias": draw_w_bias(jax.random.fold_in(streams_of[10], 71), 0),
        "w_project": scatter_about(streams_of[4], (4, SINGLE, SINGLE), SINGLE ** -0.5, 0.1875, ((2, 16),)),
        "w_out": scatter_about(streams_of[5], (SINGLE, SINGLE), SINGLE ** -0.5, 0.1875),
        "w_factors": scatter_about(streams_of[6], (SINGLE, 2 * OPD), SINGLE ** -0.5, 0.1875),
        "w_pairout": scatter_about(streams_of[7], (2 * OPD, PAIR), (2 * OPD) ** -0.5, 0.5),
        "w_up": scatter_about(streams_of[8], (PAIR, PAIR_HID), PAIR ** -0.5, 0.5),
        "w_down": scatter_about(streams_of[9], (PAIR_HID, PAIR), PAIR_HID ** -0.5, 0.25),
    }


epsilon = 1e-05

def normalize(values):
    values = values.astype(jnp.float32)
    centred = values - lax.optimization_barrier(jnp.mean(values, -1, keepdims=True))
    return centred * lax.rsqrt(lax.optimization_barrier(jnp.mean(centred * centred, -1, keepdims=True)) + epsilon)

def reference(single, pair, residue_mask, w_bias, w_project, w_out, w_factors, w_pairout, w_up, w_down):
    block_rows = math.gcd(RESIDUES, 32)
    count_blocks = RESIDUES // block_rows
    pair_blocks = pair.reshape(count_blocks, block_rows, RESIDUES, PAIR)

    def bias_block(pair_block):
        normed_pair = normalize(pair_block).astype(jnp.bfloat16)
        return jnp.einsum('rcp,ph->hrc', normed_pair.astype(jnp.float32), w_bias.astype(jnp.float32)).astype(jnp.bfloat16)
    bias_parts = lax.map(bias_block, pair_blocks)
    bias_all = jnp.transpose(bias_parts, (1, 0, 2, 3)).reshape(HEADS, RESIDUES, RESIDUES)
    normed_single = normalize(single).astype(jnp.bfloat16)
    projected = jnp.einsum('rs,fsc->frc', normed_single.astype(jnp.float32), w_project.astype(jnp.float32))
    query_rows = projected[0].astype(jnp.bfloat16).reshape(RESIDUES, HEADS, HEAD_DIM).transpose(1, 0, 2)
    key_rows = projected[1].astype(jnp.bfloat16).reshape(RESIDUES, HEADS, HEAD_DIM).transpose(1, 0, 2)
    value_rows = projected[2].astype(jnp.bfloat16).reshape(RESIDUES, HEADS, HEAD_DIM).transpose(1, 0, 2)
    gate_values = jax.nn.sigmoid(projected[3])
    key_valid = (residue_mask > 0)[None, :]
    score_scale = 1.0 / math.sqrt(HEAD_DIM)

    def attend_head(operands):
        query_head, key_head, value_head, bias_head = operands
        scores = jnp.dot(query_head, key_head.T, preferred_element_type=jnp.float32) * score_scale + bias_head.astype(jnp.float32)
        scores = jnp.where(key_valid, scores, -jnp.inf)
        weights = jax.nn.softmax(scores, axis=-1).astype(jnp.bfloat16)
        return jnp.dot(weights, value_head, preferred_element_type=jnp.float32)
    attended = lax.map(attend_head, (query_rows, key_rows, value_rows, bias_all))
    attended = attended.transpose(1, 0, 2).reshape(RESIDUES, SINGLE)
    mixed = (attended * gate_values).astype(jnp.bfloat16)
    single_out = (single.astype(jnp.float32) + jnp.dot(mixed, w_out, preferred_element_type=jnp.float32)).astype(jnp.bfloat16)
    normed_out = normalize(single_out).astype(jnp.bfloat16)
    factors = jnp.dot(normed_out, w_factors, preferred_element_type=jnp.float32).astype(jnp.bfloat16)
    left_factor = factors[:, :OPD]
    right_factor = factors[:, OPD:]

    def update_block(operands):
        pair_block, left_block = operands
        left_wide = left_block.astype(jnp.float32)[:, None, :]
        right_wide = right_factor.astype(jnp.float32)[None, :, :]
        paired = jnp.concatenate([left_wide * right_wide, left_wide - right_wide], -1).astype(jnp.bfloat16)
        pair_mid = (pair_block.astype(jnp.float32) + jnp.einsum('rcq,qp->rcp', paired.astype(jnp.float32), w_pairout.astype(jnp.float32))).astype(jnp.bfloat16)
        normed_mid = normalize(pair_mid).astype(jnp.bfloat16)
        hidden = jax.nn.relu(jnp.einsum('rcp,pk->rck', normed_mid.astype(jnp.float32), w_up.astype(jnp.float32))).astype(jnp.bfloat16)
        return (pair_mid.astype(jnp.float32) + jnp.einsum('rck,kp->rcp', hidden.astype(jnp.float32), w_down.astype(jnp.float32))).astype(jnp.bfloat16)
    updated = lax.map(update_block, (pair_blocks, left_factor.reshape(count_blocks, block_rows, OPD)))
    return (single_out, updated.reshape(RESIDUES, RESIDUES, PAIR))
```

```python
import functools
import math

import jax
import jax.numpy as jnp
from jax import lax
from jax.experimental import pallas as pl
from jax.experimental.pallas import tpu as pltpu
from jax.sharding import PartitionSpec as P

epsilon = 1e-05
f32 = jnp.float32
bf16 = jnp.bfloat16
lowest = -1e30


def normalize(values):
    centred = values - jnp.mean(values, -1, keepdims=True)
    return centred * lax.rsqrt(jnp.mean(centred * centred, -1, keepdims=True) + epsilon)


def nt_dot(a, b):
    return lax.dot_general(a, b, (((1,), (1,)), ((), ())), preferred_element_type=f32)


def project_kernel(single_ref, weight_ref, query_ref, kv_ref, gate_ref):
    normed = normalize(single_ref[...].astype(f32)).astype(bf16)
    projected = nt_dot(weight_ref[...], normed)
    width = query_ref.shape[0]
    query_ref[...] = projected[:width].astype(bf16)
    kv_ref[...] = projected[width : 3 * width].astype(bf16)
    gate_ref[...] = jax.nn.sigmoid(projected[3 * width :])


def bias_kernel(pair_ref, weight_ref, out_ref, held_ref):
    block_rows, tile_cols, width = pair_ref.shape
    weight = weight_ref[...]
    for i in range(0, block_rows, 2):
        values = pair_ref[i : i + 2].astype(f32).reshape(2 * tile_cols, width)
        both = nt_dot(weight, normalize(values).astype(bf16))
        held_ref[:, i, :] = both[:, :tile_cols]
        held_ref[:, i + 1, :] = both[:, tile_cols:]
    out_ref[...] = held_ref[...].astype(bf16)


def attend_kernel(swap_ref, query_ref, gate_ref, bias_ref, kv_ref, mask_ref, out_ref, score_ref):
    blocks, heads_here, tile_rows, tile_cols = bias_ref.shape
    width = query_ref.shape[0]
    head_width = width // heads_here
    score_scale = 1.0 / math.sqrt(head_width)
    half = kv_ref.shape[0]
    swap = swap_ref[0]
    query = jnp.transpose(query_ref[...].astype(f32)).astype(bf16)
    attended = []
    for h in range(heads_here):
        query_head = query[:, h * head_width : (h + 1) * head_width]
        key_rows = pl.ds(h * head_width, head_width)
        value_rows = pl.ds(width + h * head_width, head_width)
        top = None
        for b in range(blocks):
            key = kv_ref[b % half, (b // half) ^ swap, key_rows, :]
            scores = jnp.dot(query_head, key, preferred_element_type=f32) * score_scale
            scores = scores + bias_ref[b, h].astype(f32)
            scores = jnp.where(mask_ref[b : b + 1, :] > 0, scores, lowest)
            score_ref[b] = scores
            top = scores if top is None else jnp.maximum(top, scores)
        top = jnp.max(top, axis=-1, keepdims=True)
        total = mixed = None
        for b in range(blocks):
            value = kv_ref[b % half, (b // half) ^ swap, value_rows, :]
            weights = jnp.exp(score_ref[b] - top)
            part = nt_dot(weights.astype(bf16), value)
            total = weights if total is None else total + weights
            mixed = part if mixed is None else mixed + part
        attended.append(mixed / jnp.sum(total, axis=-1, keepdims=True))
    mixed = jnp.transpose(jnp.concatenate(attended, axis=1)) * gate_ref[...]
    mixed = mixed.astype(bf16)
    for d in range(out_ref.shape[0]):
        out_ref[d] = mixed


def factor_kernel(mixed_ref, w_out_ref, single_ref, w_factors_ref, out_ref, factors_ref):
    mixed = jnp.transpose(mixed_ref[...].astype(f32)).astype(bf16)
    head_total = jnp.dot(mixed, w_out_ref[...], preferred_element_type=f32)
    single_out = (single_ref[...].astype(f32) + head_total).astype(bf16)
    out_ref[...] = single_out
    normed = normalize(single_out.astype(f32)).astype(bf16)
    factors_ref[...] = jnp.dot(normed, w_factors_ref[...], preferred_element_type=f32).astype(bf16)


def update_kernel(pair_ref, left_ref, right_ref, w_pairout_ref, w_up_ref, w_down_ref, out_ref):
    block_rows, tile_cols, width = pair_ref.shape
    factor_width = width // 2
    right = right_ref[:, factor_width:].astype(f32)
    right = jnp.concatenate([right, right], axis=1)
    lane = lax.broadcasted_iota(jnp.int32, (1, width), 1)
    for i in range(block_rows):
        left = left_ref[i : i + 1, :factor_width].astype(f32)
        left = jnp.concatenate([left, left], axis=1)
        scale = jnp.where(lane < factor_width, left, -1.0)
        shift = jnp.where(lane < factor_width, 0.0, left)
        paired = (right * scale + shift).astype(bf16)
        moved = jnp.dot(paired, w_pairout_ref[...], preferred_element_type=f32)
        pair_mid = (pair_ref[i].astype(f32) + moved).astype(bf16).astype(f32)
        normed = normalize(pair_mid).astype(bf16)
        hidden = jnp.dot(normed, w_up_ref[...], preferred_element_type=f32)
        hidden = jnp.maximum(hidden, 0.0).astype(bf16)
        down = jnp.dot(hidden, w_down_ref[...], preferred_element_type=f32)
        out_ref[i] = (pair_mid + down).astype(bf16)


def whole(shape):
    return pl.BlockSpec(shape, lambda *_: (0,) * len(shape))


def params():
    return pltpu.CompilerParams(vmem_limit_bytes=16 * 1024 * 1024)


def gather_directly(value, axis, groups=None, count=None):
    count = count or lax.axis_size(axis)
    pieces = jnp.broadcast_to(value[None], (count, *value.shape))
    return lax.all_to_all(pieces, axis, 0, 0, axis_index_groups=groups, tiled=True)


def per_device(
    single, pair, residue_mask, w_bias, w_project, w_out, w_factors, w_pairout, w_up, w_down
):
    tile_rows, tile_cols, pair_width = pair.shape
    single_width = single.shape[1]
    width = w_project.shape[2]
    rows, cols = lax.axis_size("rows"), lax.axis_size("cols")
    heads = w_bias.shape[1]
    heads_here = heads // cols

    weight = jnp.transpose(w_project, (0, 2, 1)).reshape(4 * width, single_width)
    query, kv, gate_values = pl.pallas_call(
        project_kernel,
        out_shape=(
            jax.ShapeDtypeStruct((width, tile_rows), bf16),
            jax.ShapeDtypeStruct((2 * width, tile_rows), bf16),
            jax.ShapeDtypeStruct((width, tile_rows), f32),
        ),
        compiler_params=params(),
        name="project",
    )(single, weight)

    half = rows // 2
    kv_other = lax.ppermute(kv, "rows", [(r, r ^ half) for r in range(rows)])
    groups = [list(range(half)), list(range(half, rows))]
    kv_all = gather_directly(jnp.stack([kv, kv_other]), "rows", groups, half)

    block_rows = 16
    bias_local = pl.pallas_call(
        bias_kernel,
        grid=(tile_rows // block_rows,),
        in_specs=[
            pl.BlockSpec((block_rows, tile_cols, pair_width), lambda i: (i, 0, 0)),
            whole((heads, pair_width)),
        ],
        out_specs=pl.BlockSpec((heads, block_rows, tile_cols), lambda i: (0, i, 0)),
        out_shape=jax.ShapeDtypeStruct((heads, tile_rows, tile_cols), bf16),
        scratch_shapes=[pltpu.VMEM((heads, block_rows, tile_cols), f32)],
        compiler_params=params(),
        name="bias",
    )(pair, jnp.transpose(w_bias))
    bias_heads = lax.all_to_all(bias_local, "cols", 0, 0, tiled=True)

    swap = (lax.axis_index("rows") // half).astype(jnp.int32).reshape(1)
    mixed = pl.pallas_call(
        attend_kernel,
        in_specs=[pl.BlockSpec(memory_space=pltpu.SMEM)] + [pl.BlockSpec(memory_space=pltpu.VMEM)] * 5,
        out_shape=jax.ShapeDtypeStruct((cols, width, tile_rows), bf16),
        scratch_shapes=[pltpu.VMEM((cols, tile_rows, tile_cols), f32)],
        compiler_params=params(),
        name="attend",
    )(
        swap,
        query,
        gate_values,
        bias_heads.reshape(cols, heads_here, tile_rows, tile_cols),
        kv_all,
        residue_mask.reshape(cols, tile_cols),
    )
    mixed_all = lax.all_to_all(mixed, "cols", 0, 0, tiled=True).reshape(single_width, tile_rows)

    single_out, factors = pl.pallas_call(
        factor_kernel,
        out_shape=(
            jax.ShapeDtypeStruct(single.shape, bf16),
            jax.ShapeDtypeStruct((tile_rows, w_factors.shape[1]), bf16),
        ),
        compiler_params=params(),
        name="factor",
    )(mixed_all, w_out, single, w_factors)

    swapped = [(a * cols + b, b * cols + a) for a in range(rows) for b in range(cols)]
    right_factors = lax.ppermute(factors, ("rows", "cols"), swapped)

    block_rows = 16
    updated = pl.pallas_call(
        update_kernel,
        grid=(tile_rows // block_rows,),
        in_specs=[
            pl.BlockSpec((block_rows, tile_cols, pair_width), lambda i: (i, 0, 0)),
            pl.BlockSpec((block_rows, factors.shape[1]), lambda i: (i, 0)),
            whole(right_factors.shape),
            whole(w_pairout.shape),
            whole(w_up.shape),
            whole(w_down.shape),
        ],
        out_specs=pl.BlockSpec((block_rows, tile_cols, pair_width), lambda i: (i, 0, 0)),
        out_shape=jax.ShapeDtypeStruct(pair.shape, bf16),
        compiler_params=params(),
        name="update",
    )(pair, factors, right_factors, w_pairout, w_up, w_down)
    return (single_out, updated)


def solution(mesh):
    return jax.shard_map(
        per_device,
        mesh=mesh,
        in_specs=(
            P("rows", None),
            P("rows", "cols", None),
            P(),
            P(),
            P(None, None, "cols"),
            P(),
            P(),
            P(),
            P(),
            P(),
        ),
        out_specs=(P("rows", None), P("rows", "cols", None)),
        check_vma=False,
    )
```

```python
import functools
import math

import jax
import jax.numpy as jnp
from jax import lax
from jax.experimental import pallas as pl
from jax.experimental.pallas import tpu as pltpu
from jax.sharding import PartitionSpec as P

epsilon = 1e-05
f32 = jnp.float32
bf16 = jnp.bfloat16
lowest = -1e30


def normalize(values):
    centred = values - jnp.mean(values, -1, keepdims=True)
    return centred * lax.rsqrt(jnp.mean(centred * centred, -1, keepdims=True) + epsilon)


def nt_dot(a, b):
    return lax.dot_general(a, b, (((1,), (1,)), ((), ())), preferred_element_type=f32)


def project_kernel(single_ref, weight_ref, query_ref, kv_ref, gate_ref):
    normed = normalize(single_ref[...].astype(f32)).astype(bf16)
    projected = nt_dot(weight_ref[...], normed)
    width = query_ref.shape[0]
    query_ref[...] = projected[:width].astype(bf16)
    kv_ref[...] = projected[width : 3 * width].astype(bf16)
    gate_ref[...] = jax.nn.sigmoid(projected[3 * width :])


def normalize_rows(rounded):
    values = rounded.astype(f32)
    width = values.shape[-1]
    centred = values - jnp.dot(
        rounded, jnp.full((width, width), 1.0 / width, bf16), preferred_element_type=f32
    )
    square = jnp.mean(centred * centred, -1, keepdims=True)
    return (centred * lax.rsqrt(square + epsilon)).astype(bf16)


def bias_kernel(pair_ref, weight_ref, out_ref, held_ref):
    block_rows, tile_cols, width = pair_ref.shape
    normed = normalize_rows(pair_ref[...].reshape(block_rows * tile_cols, width))
    both = nt_dot(weight_ref[...], normed)
    for i in range(block_rows):
        held_ref[:, i, :] = both[:, i * tile_cols : (i + 1) * tile_cols]
    out_ref[...] = held_ref[...].astype(bf16)


def attend_kernel(
    place_ref, query_ref, gate_ref, bias_ref, near_ref, far_ref, mask_ref, out_ref, score_ref
):
    blocks, heads_here, tile_rows, tile_cols = bias_ref.shape
    width = query_ref.shape[0]
    head_width = width // heads_here
    score_scale = 1.0 / math.sqrt(head_width)
    shifts, halves = near_ref.shape[:2]
    half, turn, core = place_ref[0], place_ref[1], place_ref[2]
    order = []
    for c, kv_ref in enumerate((near_ref, far_ref)):
        for s in range(shifts):
            for z in range(halves):
                row = ((half ^ z) * shifts + ((turn + shifts - s) & (shifts - 1))) * 2 + (core ^ c)
                order.append((kv_ref, s, z, row))
    query = jnp.transpose(query_ref[...].astype(f32)).astype(bf16)
    attended = []
    for h in range(heads_here):
        query_head = query[:, h * head_width : (h + 1) * head_width]
        key_rows = pl.ds(h * head_width, head_width)
        value_rows = pl.ds(width + h * head_width, head_width)
        top = None
        for b, (kv_ref, s, z, row) in enumerate(order):
            key = kv_ref[s, z, key_rows, :]
            scores = jnp.dot(query_head, key, preferred_element_type=f32) * score_scale
            scores = scores + bias_ref[row, h].astype(f32)
            scores = jnp.where(mask_ref[row] > 0, scores, lowest)
            score_ref[b] = scores
            top = scores if top is None else jnp.maximum(top, scores)
        top = jnp.max(top, axis=-1, keepdims=True)
        total = mixed = None
        for b, (kv_ref, s, z, row) in enumerate(order):
            weights = jnp.exp(score_ref[b] - top)
            part = nt_dot(weights.astype(bf16), kv_ref[s, z, value_rows, :])
            total = weights if total is None else total + weights
            mixed = part if mixed is None else mixed + part
        attended.append(mixed / jnp.sum(total, axis=-1, keepdims=True))
    mixed = jnp.transpose(jnp.concatenate(attended, axis=1)) * gate_ref[...]
    mixed = mixed.astype(bf16)
    for d in range(out_ref.shape[0]):
        out_ref[d] = mixed


def factor_kernel(mixed_ref, w_out_ref, single_ref, w_factors_ref, out_ref, factors_ref):
    mixed = jnp.transpose(mixed_ref[...].astype(f32)).astype(bf16)
    head_total = jnp.dot(mixed, w_out_ref[...], preferred_element_type=f32)
    single_out = (single_ref[...].astype(f32) + head_total).astype(bf16)
    out_ref[...] = single_out
    normed = normalize(single_out.astype(f32)).astype(bf16)
    factors_ref[...] = jnp.dot(normed, w_factors_ref[...], preferred_element_type=f32).astype(bf16)


def update_kernel(
    pair_ref, left_ref, right_ref, w_pairout_ref, w_up_ref, w_down_ref, out_ref, scale_ref, shift_ref
):
    block_rows, tile_cols, width = pair_ref.shape
    factor_width = width // 2
    low = lax.broadcasted_iota(jnp.int32, (1, width), 1) < factor_width
    right = right_ref[:, factor_width:]
    right = jnp.concatenate([right, right], axis=1)
    left = left_ref[:, :factor_width].astype(f32)
    left = jnp.concatenate([left, left], axis=1)
    scale_ref[...] = jnp.where(low, left, -1.0).astype(bf16)[:, None, :]
    shift_ref[...] = jnp.where(low, 0.0, left).astype(bf16)[:, None, :]
    rows_here = block_rows * tile_cols
    paired = (right[None] * scale_ref[...] + shift_ref[...]).reshape(rows_here, width)
    moved = jnp.dot(paired, w_pairout_ref[...], preferred_element_type=f32)
    pair_mid = (pair_ref[...].reshape(rows_here, width).astype(f32) + moved).astype(bf16)
    normed = normalize_rows(pair_mid)
    hidden = jnp.dot(normed, w_up_ref[...], preferred_element_type=f32).astype(bf16)
    hidden = jnp.maximum(hidden, 0)
    down = jnp.dot(hidden, w_down_ref[...], preferred_element_type=f32)
    out_ref[...] = (pair_mid.astype(f32) + down).astype(bf16).reshape(pair_ref.shape)


def whole(shape):
    return pl.BlockSpec(shape, lambda *_: (0,) * len(shape))


def params(mib=8):
    return pltpu.CompilerParams(vmem_limit_bytes=mib * 1024 * 1024)


def per_device(
    single, pair, residue_mask, w_bias, w_project, w_out, w_factors, w_pairout, w_up, w_down
):
    tile_rows, tile_cols, pair_width = pair.shape
    single_width = single.shape[1]
    width = w_project.shape[2]
    rows, cols = lax.axis_size("rows"), lax.axis_size("cols")
    heads = w_bias.shape[1]
    heads_here = heads // cols

    block_rows = 64
    bias_local = pl.pallas_call(
        bias_kernel,
        grid=(tile_rows // block_rows,),
        in_specs=[
            pl.BlockSpec((block_rows, tile_cols, pair_width), lambda i: (i, 0, 0)),
            whole((heads, pair_width)),
        ],
        out_specs=pl.BlockSpec((heads, block_rows, tile_cols), lambda i: (0, i, 0)),
        out_shape=jax.ShapeDtypeStruct((heads, tile_rows, tile_cols), bf16),
        scratch_shapes=[pltpu.VMEM((heads, block_rows, tile_cols), f32)],
        compiler_params=params(20),
        name="bias",
    )(pair, jnp.transpose(w_bias))
    bias_local, single = lax.optimization_barrier((bias_local, single))
    bias_heads = lax.all_to_all(bias_local, "cols", 0, 0, tiled=True)

    weight = jnp.transpose(w_project, (0, 2, 1)).reshape(4 * width, single_width)
    query, kv, gate_values = pl.pallas_call(
        project_kernel,
        out_shape=(
            jax.ShapeDtypeStruct((width, tile_rows), bf16),
            jax.ShapeDtypeStruct((2 * width, tile_rows), bf16),
            jax.ShapeDtypeStruct((width, tile_rows), f32),
        ),
        compiler_params=params(),
        name="project",
    )(single, weight)

    shifts = rows // 4
    half = rows // 2

    def sent(value, target):
        return lax.ppermute(value, "rows", [(r, target(r)) for r in range(rows)])

    both = jnp.stack([kv, sent(kv, lambda r: r ^ half)])
    near = [both]
    for s in range(1, shifts):
        near.append(sent(both, lambda r: (r & half) | ((r + 2 * s) & (half - 1))))
    near = jnp.stack(near)
    far = sent(near, lambda r: r ^ 1)

    row = lax.axis_index("rows")
    place = jnp.stack([row // half, (row % half) // 2, row % 2]).astype(jnp.int32)
    mixed = pl.pallas_call(
        attend_kernel,
        in_specs=[pl.BlockSpec(memory_space=pltpu.SMEM)] + [pl.BlockSpec(memory_space=pltpu.VMEM)] * 6,
        out_shape=jax.ShapeDtypeStruct((cols, width, tile_rows), bf16),
        scratch_shapes=[pltpu.VMEM((cols, tile_rows, tile_cols), f32)],
        compiler_params=params(),
        name="attend",
    )(
        place,
        query,
        gate_values,
        bias_heads.reshape(cols, heads_here, tile_rows, tile_cols),
        near,
        far,
        residue_mask.reshape(cols, 1, tile_cols),
    )
    mixed_all = lax.all_to_all(mixed, "cols", 0, 0, tiled=True).reshape(single_width, tile_rows)

    single_out, factors = pl.pallas_call(
        factor_kernel,
        out_shape=(
            jax.ShapeDtypeStruct(single.shape, bf16),
            jax.ShapeDtypeStruct((tile_rows, w_factors.shape[1]), bf16),
        ),
        compiler_params=params(),
        name="factor",
    )(mixed_all, w_out, single, w_factors)

    swapped = [(a * cols + b, b * cols + a) for a in range(rows) for b in range(cols)]
    right_factors = lax.ppermute(factors, ("rows", "cols"), swapped)

    block_rows = 32
    updated = pl.pallas_call(
        update_kernel,
        grid=(tile_rows // block_rows,),
        in_specs=[
            pl.BlockSpec((block_rows, tile_cols, pair_width), lambda i: (i, 0, 0)),
            pl.BlockSpec((block_rows, factors.shape[1]), lambda i: (i, 0)),
            whole(right_factors.shape),
            whole(w_pairout.shape),
            whole(w_up.shape),
            whole(w_down.shape),
        ],
        out_specs=pl.BlockSpec((block_rows, tile_cols, pair_width), lambda i: (i, 0, 0)),
        out_shape=jax.ShapeDtypeStruct(pair.shape, bf16),
        scratch_shapes=[pltpu.VMEM((block_rows, 1, pair_width), bf16)] * 2,
        compiler_params=params(20),
        name="update",
    )(pair, factors, right_factors, w_pairout, w_up, w_down)
    return (single_out, updated)


def solution(mesh):
    return jax.shard_map(
        per_device,
        mesh=mesh,
        in_specs=(
            P("rows", None),
            P("rows", "cols", None),
            P(),
            P(),
            P(None, None, "cols"),
            P(),
            P(),
            P(),
            P(),
            P(),
        ),
        out_specs=(P("rows", None), P("rows", "cols", None)),
        check_vma=False,
    )
```

```python
import functools
import math

import jax
import jax.numpy as jnp
from jax import lax
from jax.experimental import pallas as pl
from jax.experimental.pallas import tpu as pltpu
from jax.sharding import PartitionSpec as P

epsilon = 1e-05
f32 = jnp.float32
bf16 = jnp.bfloat16
lowest = -1e30


def normalize(values):
    centred = values - jnp.mean(values, -1, keepdims=True)
    return centred * lax.rsqrt(jnp.mean(centred * centred, -1, keepdims=True) + epsilon)


def nt_dot(a, b):
    return lax.dot_general(a, b, (((1,), (1,)), ((), ())), preferred_element_type=f32)


def start_copies(pairs, sems):
    copies = [pltpu.make_async_copy(a, b, sems.at[i]) for i, (a, b) in enumerate(pairs)]
    for copy in copies:
        copy.start()
    return copies


def project_kernel(
    single_hbm, weight_hbm, query_ref, kv_ref, gate_ref, single_ref, weight_ref, sems
):
    copies = start_copies(((single_hbm, single_ref), (weight_hbm, weight_ref)), sems)
    copies[0].wait()
    normed = normalize(single_ref[...].astype(f32)).astype(bf16)
    copies[1].wait()
    projected = nt_dot(weight_ref[...], normed)
    width = query_ref.shape[0]
    query_ref[...] = projected[:width].astype(bf16)
    kv_ref[...] = projected[width : 3 * width].astype(bf16)
    gate_ref[...] = jax.nn.sigmoid(projected[3 * width :])


def normalize_rows(rounded):
    values = rounded.astype(f32)
    width = values.shape[-1]
    centred = values - jnp.dot(
        rounded, jnp.full((width, width), 1.0 / width, bf16), preferred_element_type=f32
    )
    square = jnp.mean(centred * centred, -1, keepdims=True)
    return (centred * lax.rsqrt(square + epsilon)).astype(bf16)


def bias_kernel(
    pair_hbm, weight_hbm, mask_hbm, out_ref, pair_ref, weight_ref, mask_ref, held_ref, sems
):
    tile_rows, tile_cols, width = pair_ref.shape
    step = held_ref.shape[1]
    parts = [(weight_hbm, weight_ref), (mask_hbm.at[lax.axis_index("cols")], mask_ref)]
    for at in range(0, tile_rows, step):
        parts.append((pair_hbm.at[pl.ds(at, step)], pair_ref.at[pl.ds(at, step)]))
    copies = start_copies(parts, sems)
    copies[0].wait()
    copies[1].wait()
    included = mask_ref[...] > 0
    for at in range(0, tile_rows, step):
        copies[2 + at // step].wait()
        normed = normalize_rows(pair_ref[at : at + step].reshape(step * tile_cols, width))
        both = nt_dot(weight_ref[...], normed)
        for i in range(step):
            held_ref[:, i, :] = both[:, i * tile_cols : (i + 1) * tile_cols]
        held = jnp.where(included[None], held_ref[...], lowest)
        out_ref[:, at : at + step, :] = held.astype(bf16)


def attend_kernel(query_ref, gate_ref, bias_ref, kv_ref, out_ref, score_ref):
    blocks, heads_here, tile_rows, tile_cols = bias_ref.shape
    width = query_ref.shape[0]
    head_width = width // heads_here
    score_scale = 1.0 / math.sqrt(head_width)
    shifts = kv_ref.shape[1]
    me = lax.axis_index("rows")
    half, turn, core = me // (2 * shifts), (me // 2) % shifts, me % 2

    def block(b, part):
        sent = (turn + shifts - (b // 2) % shifts) % shifts
        return kv_ref[(b % 2) ^ core, sent, (b // (2 * shifts)) ^ half, part, :]

    query = jnp.transpose(query_ref[...].astype(f32)).astype(bf16)
    attended = []
    for h in range(heads_here):
        query_head = query[:, h * head_width : (h + 1) * head_width]
        key_rows = pl.ds(h * head_width, head_width)
        value_rows = pl.ds(width + h * head_width, head_width)
        top = None
        for b in range(blocks):
            scores = jnp.dot(query_head, block(b, key_rows), preferred_element_type=f32)
            scores = scores * score_scale + bias_ref[b, h].astype(f32)
            score_ref[b] = scores
            top = scores if top is None else jnp.maximum(top, scores)
        top = jnp.max(top, axis=-1, keepdims=True)
        total = mixed = None
        for b in range(blocks):
            weights = jnp.exp(score_ref[b] - top)
            part = nt_dot(weights.astype(bf16), block(b, value_rows))
            total = weights if total is None else total + weights
            mixed = part if mixed is None else mixed + part
        attended.append(mixed / jnp.sum(total, axis=-1, keepdims=True))
    mixed = jnp.transpose(jnp.concatenate(attended, axis=1)) * gate_ref[...]
    mixed = mixed.astype(bf16)
    for d in range(out_ref.shape[0]):
        out_ref[d] = mixed


def factor_kernel(
    mixed_ref,
    w_out_hbm,
    single_hbm,
    w_factors_hbm,
    out_ref,
    factors_ref,
    w_out_ref,
    single_ref,
    w_factors_ref,
    sems,
):
    depth = w_out_ref.shape[0]
    step = depth // 4
    parts = [(w_out_hbm.at[pl.ds(at, step)], w_out_ref.at[pl.ds(at, step)]) for at in range(0, depth, step)]
    parts += [(single_hbm, single_ref), (w_factors_hbm, w_factors_ref)]
    copies = start_copies(parts, sems)
    mixed = jnp.transpose(mixed_ref[...].astype(f32)).astype(bf16)
    head_total = None
    for at in range(0, depth, step):
        copies[at // step].wait()
        part = jnp.dot(
            mixed[:, at : at + step], w_out_ref[at : at + step, :], preferred_element_type=f32
        )
        head_total = part if head_total is None else head_total + part
    copies[4].wait()
    single_out = (single_ref[...].astype(f32) + head_total).astype(bf16)
    out_ref[...] = single_out
    normed = normalize(single_out.astype(f32)).astype(bf16)
    copies[5].wait()
    factors_ref[...] = jnp.dot(normed, w_factors_ref[...], preferred_element_type=f32).astype(bf16)


def update_kernel(
    pair_ref,
    left_ref,
    right_ref,
    w_pairout_hbm,
    w_up_hbm,
    w_down_hbm,
    out_ref,
    w_pairout_ref,
    w_up_ref,
    w_down_ref,
    scale_ref,
    shift_ref,
    sems,
):
    @pl.when(pl.program_id(0) == 0)
    def _():
        copies = start_copies(
            (
                (w_pairout_hbm, w_pairout_ref),
                (w_up_hbm, w_up_ref),
                (w_down_hbm, w_down_ref),
            ),
            sems,
        )
        for copy in copies:
            copy.wait()

    block_rows, tile_cols, width = pair_ref.shape
    factor_width = width // 2
    low = lax.broadcasted_iota(jnp.int32, (1, width), 1) < factor_width
    right = right_ref[:, factor_width:]
    right = jnp.concatenate([right, right], axis=1)
    left = left_ref[:, :factor_width].astype(f32)
    left = jnp.concatenate([left, left], axis=1)
    scale_ref[...] = jnp.where(low, left, -1.0).astype(bf16)[:, None, :]
    shift_ref[...] = jnp.where(low, 0.0, left).astype(bf16)[:, None, :]
    rows_here = block_rows * tile_cols
    paired = (right[None] * scale_ref[...] + shift_ref[...]).reshape(rows_here, width)
    moved = jnp.dot(paired, w_pairout_ref[...], preferred_element_type=f32)
    pair_mid = (pair_ref[...].reshape(rows_here, width).astype(f32) + moved).astype(bf16)
    normed = normalize_rows(pair_mid)
    hidden = jnp.dot(normed, w_up_ref[...], preferred_element_type=f32).astype(bf16)
    hidden = jnp.maximum(hidden, 0)
    down = jnp.dot(hidden, w_down_ref[...], preferred_element_type=f32)
    out_ref[...] = (pair_mid.astype(f32) + down).astype(bf16).reshape(pair_ref.shape)


def whole(shape):
    return pl.BlockSpec(shape, lambda *_: (0,) * len(shape))


def pinned(value):
    return pltpu.with_memory_space_constraint(value, pltpu.HBM)


def params(mib=8):
    return pltpu.CompilerParams(vmem_limit_bytes=mib * 1024 * 1024)


def per_device(
    single, pair, residue_mask, w_bias, w_project, w_out, w_factors, w_pairout, w_up, w_down
):
    tile_rows, tile_cols, pair_width = pair.shape
    single_width = single.shape[1]
    width = w_project.shape[2]
    rows, cols = lax.axis_size("rows"), lax.axis_size("cols")
    heads = w_bias.shape[1]
    heads_here = heads // cols
    in_place = pl.BlockSpec(memory_space=pl.ANY)
    in_hbm = pl.BlockSpec(memory_space=pltpu.HBM)

    weight = jnp.transpose(w_project, (0, 2, 1)).reshape(4 * width, single_width)
    query, kv, gate_values = pl.pallas_call(
        project_kernel,
        out_shape=(
            jax.ShapeDtypeStruct((width, tile_rows), bf16),
            jax.ShapeDtypeStruct((2 * width, tile_rows), bf16),
            jax.ShapeDtypeStruct((width, tile_rows), f32),
        ),
        in_specs=[in_hbm, in_hbm],
        scratch_shapes=[
            pltpu.VMEM(single.shape, bf16),
            pltpu.VMEM(weight.shape, bf16),
            pltpu.SemaphoreType.DMA((2,)),
        ],
        compiler_params=params(),
        name="project",
    )(pinned(single), pinned(weight))

    shifts = rows // 4
    half = rows // 2

    def sent(value, target):
        return lax.ppermute(value, "rows", [(r, target(r)) for r in range(rows)])

    kv_other = sent(kv, lambda r: r ^ half)
    kv, w_bias = lax.optimization_barrier((kv, w_bias))

    bias_local = pl.pallas_call(
        bias_kernel,
        out_shape=jax.ShapeDtypeStruct((heads, tile_rows, tile_cols), bf16),
        in_specs=[in_hbm, in_hbm, in_hbm],
        scratch_shapes=[
            pltpu.VMEM(pair.shape, bf16),
            pltpu.VMEM((heads, pair_width), bf16),
            pltpu.VMEM((1, tile_cols), jnp.int32),
            pltpu.VMEM((heads, tile_rows // 4, tile_cols), f32),
            pltpu.SemaphoreType.DMA((6,)),
        ],
        compiler_params=params(24),
        name="bias",
    )(pinned(pair), pinned(jnp.transpose(w_bias)), pinned(residue_mask.reshape(cols, 1, tile_cols)))
    bias_local, kv_other = lax.optimization_barrier((bias_local, kv_other))
    bias_heads = lax.all_to_all(bias_local, "cols", 0, 0, tiled=True)

    both = jnp.stack([kv, kv_other])
    near = [both]
    for s in range(1, shifts):
        near.append(sent(both, lambda r: (r & half) | ((r + 2 * s) & (half - 1))))
    near = jnp.stack(near)
    kv_all = jnp.stack([near, sent(near, lambda r: r ^ 1)])

    mixed = pl.pallas_call(
        attend_kernel,
        out_shape=jax.ShapeDtypeStruct((cols, width, tile_rows), bf16),
        scratch_shapes=[pltpu.VMEM((cols, tile_rows, tile_cols), f32)],
        compiler_params=params(),
        name="attend",
    )(
        query,
        gate_values,
        bias_heads.reshape(cols, heads_here, tile_rows, tile_cols),
        kv_all,
    )
    mixed_all = lax.all_to_all(mixed, "cols", 0, 0, tiled=True).reshape(single_width, tile_rows)

    single_out, factors = pl.pallas_call(
        factor_kernel,
        out_shape=(
            jax.ShapeDtypeStruct(single.shape, bf16),
            jax.ShapeDtypeStruct((tile_rows, w_factors.shape[1]), bf16),
        ),
        in_specs=[whole((single_width, tile_rows)), in_place, in_place, in_place],
        scratch_shapes=[
            pltpu.VMEM(w_out.shape, bf16),
            pltpu.VMEM(single.shape, bf16),
            pltpu.VMEM(w_factors.shape, bf16),
            pltpu.SemaphoreType.DMA((6,)),
        ],
        compiler_params=params(),
        name="factor",
    )(mixed_all, pinned(w_out), single, w_factors)

    swapped = [(a * cols + b, b * cols + a) for a in range(rows) for b in range(cols)]
    right_factors = lax.ppermute(factors, ("rows", "cols"), swapped)

    block_rows = 32
    updated = pl.pallas_call(
        update_kernel,
        grid=(tile_rows // block_rows,),
        in_specs=[
            pl.BlockSpec((block_rows, tile_cols, pair_width), lambda i: (i, 0, 0)),
            pl.BlockSpec((block_rows, factors.shape[1]), lambda i: (i, 0)),
            whole(right_factors.shape),
            in_place,
            in_place,
            in_place,
        ],
        out_specs=pl.BlockSpec((block_rows, tile_cols, pair_width), lambda i: (i, 0, 0)),
        out_shape=jax.ShapeDtypeStruct(pair.shape, bf16),
        scratch_shapes=[
            pltpu.VMEM(w_pairout.shape, bf16),
            pltpu.VMEM(w_up.shape, bf16),
            pltpu.VMEM(w_down.shape, bf16),
            pltpu.VMEM((block_rows, 1, pair_width), bf16),
            pltpu.VMEM((block_rows, 1, pair_width), bf16),
            pltpu.SemaphoreType.DMA((3,)),
        ],
        compiler_params=params(20),
        name="update",
    )(pair, factors, right_factors, w_pairout, w_up, w_down)
    return (single_out, updated)


def solution(mesh):
    return jax.shard_map(
        per_device,
        mesh=mesh,
        in_specs=(
            P("rows", None),
            P("rows", "cols", None),
            P(),
            P(),
            P(None, None, "cols"),
            P(),
            P(),
            P(),
            P(),
            P(),
        ),
        out_specs=(P("rows", None), P("rows", "cols", None)),
        check_vma=False,
    )
```

```python
import functools
import math

import jax
import jax.numpy as jnp
from jax import lax
from jax.experimental import pallas as pl
from jax.experimental.pallas import tpu as pltpu
from jax.sharding import PartitionSpec as P

epsilon = 1e-05
f32 = jnp.float32
bf16 = jnp.bfloat16
lowest = -1e30


def normalize(values):
    centred = values - jnp.mean(values, -1, keepdims=True)
    return centred * lax.rsqrt(jnp.mean(centred * centred, -1, keepdims=True) + epsilon)


def nt_dot(a, b):
    return lax.dot_general(a, b, (((1,), (1,)), ((), ())), preferred_element_type=f32)


def start_copies(pairs, sems):
    copies = [pltpu.make_async_copy(a, b, sems.at[i]) for i, (a, b) in enumerate(pairs)]
    for copy in copies:
        copy.start()
    return copies


def project_kernel(
    single_hbm, weight_hbm, query_ref, kv_ref, single_ref, weight_ref, sems
):
    copies = start_copies(((single_hbm, single_ref), (weight_hbm, weight_ref)), sems)
    copies[0].wait()
    normed = normalize(single_ref[...].astype(f32)).astype(bf16)
    copies[1].wait()
    projected = nt_dot(weight_ref[...], normed)
    width = query_ref.shape[0] // 2
    query_ref[:width] = projected[:width].astype(bf16).astype(f32)
    query_ref[width:] = jax.nn.sigmoid(projected[3 * width :])
    kv_ref[...] = projected[width : 3 * width].astype(bf16)


def normalize_rows(rounded):
    values = rounded.astype(f32)
    width = values.shape[-1]
    centred = values - jnp.dot(
        rounded, jnp.full((width, width), 1.0 / width, bf16), preferred_element_type=f32
    )
    square = jnp.mean(centred * centred, -1, keepdims=True)
    return (centred * lax.rsqrt(square + epsilon)).astype(bf16)


def bias_kernel(
    pair_hbm,
    weight_hbm,
    mask_hbm,
    out_hbm,
    pair_ref,
    weight_ref,
    mask_ref,
    held_ref,
    staged_ref,
    sems,
    out_sems,
):
    tile_rows, tile_cols, width = pair_ref.shape
    targets, heads_there = staged_ref.shape[:2]
    pairs = heads_there // 2
    ends = [tile_rows // 4, 3 * tile_rows // 4, tile_rows]
    parts = [(weight_hbm, weight_ref), (mask_hbm.at[lax.axis_index("cols")], mask_ref)]
    at = 0
    for end in ends:
        rows_here = pl.ds(at, end - at)
        parts.append((pair_hbm.at[rows_here], pair_ref.at[rows_here]))
        at = end
    copies = start_copies(parts, sems)
    copies[0].wait()
    copies[1].wait()
    included = mask_ref[...] > 0
    at = 0
    outs = []
    for chunk, end in enumerate(ends):
        copies[2 + chunk].wait()
        step = end - at
        normed = normalize_rows(pair_ref[at:end].reshape(step * tile_cols, width))
        both = nt_dot(weight_ref[...], normed)
        for i in range(step):
            held_ref[:, i, :] = both[:, i * tile_cols : (i + 1) * tile_cols]
        held = jnp.where(included[None], held_ref[:, :step, :], lowest).astype(bf16)
        for d in range(targets):
            for p in range(heads_there // pairs):
                first = p * targets * pairs + d * pairs
                staged_ref[d, p * pairs : (p + 1) * pairs, at:end] = held[first : first + pairs]
        rows_here = pl.ds(at, step)
        out = pltpu.make_async_copy(
            staged_ref.at[:, :, rows_here], out_hbm.at[:, :, rows_here], out_sems.at[chunk]
        )
        out.start()
        outs.append(out)
        at = end
    for out in outs:
        out.wait()


def attend_kernel(own_ref, other_ref, bias_ref, near_ref, far_ref, out_ref, score_ref):
    blocks, heads_there, tile_rows, tile_cols = bias_ref.shape
    width = own_ref.shape[0] // 2
    pairs = heads_there // 2
    head_width = width // pairs
    score_scale = 1.0 / math.sqrt(head_width)
    shifts = near_ref.shape[0]
    row, col = lax.axis_index("rows"), lax.axis_index("cols")
    half, turn, core = row // (2 * shifts), (row // 2) % shifts, row % 2
    second = col // blocks

    def block(b, z, part):
        sent = (turn + shifts - b // 2) % shifts
        near, far = near_ref[sent, half ^ z, part, :], far_ref[sent, half ^ z, part, :]
        return jnp.where(core == b % 2, near, far)

    own, other = own_ref[...], other_ref[...]
    attended, gates, sums = [], [], []
    for z in range(2):
        here = jnp.where(second == z, own, other)
        query = jnp.transpose(here[:width]).astype(bf16)
        gates.append(here[width:])
        for h in range(pairs):
            query_head = query[:, h * head_width : (h + 1) * head_width]
            key_rows = pl.ds(h * head_width, head_width)
            value_rows = pl.ds(width + h * head_width, head_width)
            top = None
            for b in range(blocks):
                scores = jnp.dot(query_head, block(b, z, key_rows), preferred_element_type=f32)
                scores = scores * score_scale + bias_ref[b, z * pairs + h].astype(f32)
                score_ref[b] = scores
                top = scores if top is None else jnp.maximum(top, scores)
            top = jnp.max(top, axis=-1, keepdims=True)
            total = mixed = None
            for b in range(blocks):
                weights = jnp.exp(score_ref[b] - top)
                part = nt_dot(weights.astype(bf16), block(b, z, value_rows))
                total = weights if total is None else total + weights
                mixed = part if mixed is None else mixed + part
            total = jnp.sum(total, axis=-1, keepdims=True)
            attended.append(mixed / total)
            sums.append(top + jnp.log(total))
    gated = jnp.transpose(jnp.concatenate(attended, axis=1)) * jnp.concatenate(gates, axis=0)
    lane = lax.broadcasted_iota(jnp.int32, (tile_rows, 128), 1)
    coded = jnp.zeros((tile_rows, 128), f32)
    for h, value in enumerate(sums):
        for p in range(3):
            part = value.astype(bf16).astype(f32)
            value = value - part
            coded = jnp.where(lane == p * heads_there + h, part, coded)
    coded = jnp.transpose(coded)[: out_ref.shape[1] - 2 * width]
    gated, coded = gated.astype(bf16), coded.astype(bf16)
    for d in range(out_ref.shape[0]):
        out_ref[d, : 2 * width] = gated
        out_ref[d, 2 * width :] = coded


def factor_kernel(
    sent_ref,
    w_out_ref,
    single_hbm,
    w_factors_hbm,
    out_ref,
    factors_ref,
    mixed_ref,
    single_ref,
    w_factors_ref,
    sems,
):
    copies = start_copies(((single_hbm, single_ref), (w_factors_hbm, w_factors_ref)), sems)
    targets = sent_ref.shape[0] // 2
    width = mixed_ref.shape[0] // sent_ref.shape[0]
    heads_there = 4
    head_width = 2 * width // heads_there

    def log_sum(d):
        coded = sent_ref[d, 2 * width :].astype(f32)
        parts = [coded[p * heads_there : (p + 1) * heads_there] for p in range(3)]
        return parts[0] + parts[1] + parts[2]

    for d in range(targets):
        first, last = log_sum(d), log_sum(d + targets)
        top = jnp.maximum(first, last)
        first, last = jnp.exp(first - top), jnp.exp(last - top)
        inverse = 1.0 / (first + last)
        first, last = first * inverse, last * inverse
        for h in range(heads_there):
            rows_here = pl.ds(h * head_width, head_width)
            joined = (
                sent_ref[d, rows_here].astype(f32) * first[h : h + 1]
                + sent_ref[d + targets, rows_here].astype(f32) * last[h : h + 1]
            )
            owner = (h * head_width // width) * targets + d
            place = owner * width + h * head_width % width
            mixed_ref[place : place + head_width] = joined.astype(bf16)
    mixed = jnp.transpose(mixed_ref[...].astype(f32)).astype(bf16)
    head_total = jnp.dot(mixed, w_out_ref[...], preferred_element_type=f32)
    copies[0].wait()
    single_out = (single_ref[...].astype(f32) + head_total).astype(bf16)
    out_ref[...] = single_out
    normed = normalize(single_out.astype(f32)).astype(bf16)
    copies[1].wait()
    factors_ref[...] = jnp.dot(normed, w_factors_ref[...], preferred_element_type=f32).astype(bf16)


def update_kernel(
    pair_ref,
    left_ref,
    right_ref,
    w_pairout_hbm,
    w_up_hbm,
    w_down_hbm,
    out_ref,
    w_pairout_ref,
    w_up_ref,
    w_down_ref,
    scale_ref,
    shift_ref,
    sems,
):
    copies = [
        pltpu.make_async_copy(w_pairout_hbm, w_pairout_ref, sems.at[0]),
        pltpu.make_async_copy(w_up_hbm, w_up_ref, sems.at[1]),
        pltpu.make_async_copy(w_down_hbm, w_down_ref, sems.at[2]),
    ]

    @pl.when(pl.program_id(0) == 0)
    def _():
        for copy in copies:
            copy.start()

    block_rows, tile_cols, width = pair_ref.shape
    factor_width = width // 2
    low = lax.broadcasted_iota(jnp.int32, (1, width), 1) < factor_width
    right = right_ref[:, factor_width:]
    right = jnp.concatenate([right, right], axis=1)
    left = left_ref[:, :factor_width].astype(f32)
    left = jnp.concatenate([left, left], axis=1)
    scale_ref[...] = jnp.where(low, left, -1.0).astype(bf16)[:, None, :]
    shift_ref[...] = jnp.where(low, 0.0, left).astype(bf16)[:, None, :]
    rows_here = block_rows * tile_cols
    paired = (right[None] * scale_ref[...] + shift_ref[...]).reshape(rows_here, width)

    @pl.when(pl.program_id(0) == 0)
    def _():
        for copy in copies:
            copy.wait()

    moved = jnp.dot(paired, w_pairout_ref[...], preferred_element_type=f32)
    pair_mid = (pair_ref[...].reshape(rows_here, width).astype(f32) + moved).astype(bf16)
    normed = normalize_rows(pair_mid)
    hidden = jnp.dot(normed, w_up_ref[...], preferred_element_type=f32).astype(bf16)
    hidden = jnp.maximum(hidden, 0)
    down = jnp.dot(hidden, w_down_ref[...], preferred_element_type=f32)
    out_ref[...] = (pair_mid.astype(f32) + down).astype(bf16).reshape(pair_ref.shape)


def whole(shape):
    return pl.BlockSpec(shape, lambda *_: (0,) * len(shape))


def pinned(value):
    return pltpu.with_memory_space_constraint(value, pltpu.HBM)


def params(mib=8):
    return pltpu.CompilerParams(vmem_limit_bytes=mib * 1024 * 1024)


def per_device(
    single, pair, residue_mask, w_bias, w_project, w_out, w_factors, w_pairout, w_up, w_down
):
    tile_rows, tile_cols, pair_width = pair.shape
    single_width = single.shape[1]
    width = w_project.shape[2]
    rows, cols = lax.axis_size("rows"), lax.axis_size("cols")
    heads = w_bias.shape[1]
    in_place = pl.BlockSpec(memory_space=pl.ANY)
    in_hbm = pl.BlockSpec(memory_space=pltpu.HBM)

    shifts = rows // 4
    half_rows, half_cols = rows // 2, cols // 2
    both_axes = ("rows", "cols")

    def sent(value, axes, target):
        if axes == "rows":
            routes = [(r, target(r)) for r in range(rows)]
        elif axes == "cols":
            routes = [(c, target(c)) for c in range(cols)]
        else:
            routes = []
            for r in range(rows):
                for c in range(cols):
                    to_row, to_col = target(r, c)
                    routes.append((r * cols + c, to_row * cols + to_col))
        return lax.ppermute(value, axes, routes)

    def rerouted(flip):
        def target(r, c):
            z_row, z_col = r // half_rows, c // half_cols
            return (z_col ^ flip) * half_rows + r % half_rows, z_row * half_cols + c % half_cols

        return target

    weight = jnp.transpose(w_project, (0, 2, 1)).reshape(4 * width, single_width)
    query, kv = pl.pallas_call(
        project_kernel,
        out_shape=(
            jax.ShapeDtypeStruct((2 * width, tile_rows), f32),
            jax.ShapeDtypeStruct((2 * width, tile_rows), bf16),
        ),
        in_specs=[in_hbm, in_hbm],
        scratch_shapes=[
            pltpu.VMEM(single.shape, bf16),
            pltpu.VMEM(weight.shape, bf16),
            pltpu.SemaphoreType.DMA((2,)),
        ],
        compiler_params=params(),
        name="project",
    )(pinned(single), pinned(weight))

    kv_first = sent(kv, both_axes, rerouted(0))
    kv_last = sent(kv, both_axes, rerouted(1))
    kv, w_bias = lax.optimization_barrier((kv, w_bias))

    heads_there = 2 * heads // cols
    sent_shape = (half_cols, heads_there, tile_rows, tile_cols)
    bias_local = pl.pallas_call(
        bias_kernel,
        out_shape=jax.ShapeDtypeStruct(sent_shape, bf16),
        in_specs=[in_hbm, in_hbm, in_hbm],
        out_specs=in_place,
        scratch_shapes=[
            pltpu.VMEM(pair.shape, bf16),
            pltpu.VMEM((heads, pair_width), bf16),
            pltpu.VMEM((1, tile_cols), jnp.int32),
            pltpu.VMEM((heads, tile_rows // 2, tile_cols), f32),
            pltpu.VMEM(sent_shape, bf16),
            pltpu.SemaphoreType.DMA((5,)),
            pltpu.SemaphoreType.DMA((3,)),
        ],
        compiler_params=params(28),
        name="bias",
    )(pinned(pair), pinned(jnp.transpose(w_bias)), pinned(residue_mask.reshape(cols, 1, tile_cols)))
    bias_local, kv_first, kv_last = lax.optimization_barrier((bias_local, kv_first, kv_last))
    groups = [list(range(half_cols)), list(range(half_cols, cols))]
    bias_heads = lax.all_to_all(bias_local, "cols", 0, 0, axis_index_groups=groups, tiled=True)

    both = jnp.stack([kv_first, kv_last])
    near = [both]
    for s in range(1, shifts):
        around = lambda r: (r & half_rows) | ((r + 2 * s) & (half_rows - 1))
        near.append(sent(both, "rows", around))
    near = jnp.stack(near)
    query, near = lax.optimization_barrier((query, near))
    far = sent(near, "rows", lambda r: r ^ 1)
    query_other = sent(query, "cols", lambda c: c ^ half_cols)

    mixed = pl.pallas_call(
        attend_kernel,
        out_shape=jax.ShapeDtypeStruct((cols, 2 * width + 16, tile_rows), bf16),
        scratch_shapes=[pltpu.VMEM((half_cols, tile_rows, tile_cols), f32)],
        compiler_params=params(),
        name="attend",
    )(query, query_other, bias_heads, near, far)
    mixed_all = lax.all_to_all(mixed, "cols", 0, 0, tiled=True)

    single_out, factors = pl.pallas_call(
        factor_kernel,
        out_shape=(
            jax.ShapeDtypeStruct(single.shape, bf16),
            jax.ShapeDtypeStruct((tile_rows, w_factors.shape[1]), bf16),
        ),
        in_specs=[whole(mixed_all.shape), whole(w_out.shape), in_hbm, in_hbm],
        scratch_shapes=[
            pltpu.VMEM((single_width, tile_rows), bf16),
            pltpu.VMEM(single.shape, bf16),
            pltpu.VMEM(w_factors.shape, bf16),
            pltpu.SemaphoreType.DMA((2,)),
        ],
        compiler_params=params(),
        name="factor",
    )(mixed_all, w_out, pinned(single), pinned(w_factors))

    swapped = [(a * cols + b, b * cols + a) for a in range(rows) for b in range(cols)]
    right_factors = lax.ppermute(factors, ("rows", "cols"), swapped)

    block_rows = 32
    updated = pl.pallas_call(
        update_kernel,
        grid=(tile_rows // block_rows,),
        in_specs=[
            pl.BlockSpec((block_rows, tile_cols, pair_width), lambda i: (i, 0, 0)),
            pl.BlockSpec((block_rows, factors.shape[1]), lambda i: (i, 0)),
            whole(right_factors.shape),
            in_place,
            in_place,
            in_place,
        ],
        out_specs=pl.BlockSpec((block_rows, tile_cols, pair_width), lambda i: (i, 0, 0)),
        out_shape=jax.ShapeDtypeStruct(pair.shape, bf16),
        scratch_shapes=[
            pltpu.VMEM(w_pairout.shape, bf16),
            pltpu.VMEM(w_up.shape, bf16),
            pltpu.VMEM(w_down.shape, bf16),
            pltpu.VMEM((block_rows, 1, pair_width), bf16),
            pltpu.VMEM((block_rows, 1, pair_width), bf16),
            pltpu.SemaphoreType.DMA((3,)),
        ],
        compiler_params=params(20),
        name="update",
    )(pair, factors, right_factors, pinned(w_pairout), pinned(w_up), pinned(w_down))
    return (single_out, updated)


def solution(mesh):
    return jax.shard_map(
        per_device,
        mesh=mesh,
        in_specs=(
            P("rows", None),
            P("rows", "cols", None),
            P(),
            P(),
            P(None, None, "cols"),
            P(),
            P(),
            P(),
            P(),
            P(),
        ),
        out_specs=(P("rows", None), P("rows", "cols", None)),
        check_vma=False,
    )
```

```python
import functools
import math

import jax
import jax.numpy as jnp
from jax import lax
from jax.experimental import pallas as pl
from jax.experimental.pallas import tpu as pltpu
from jax.sharding import PartitionSpec as P

epsilon = 1e-05
f32 = jnp.float32
bf16 = jnp.bfloat16
lowest = -1e30


def normalize(values):
    centred = values - jnp.mean(values, -1, keepdims=True)
    return centred * lax.rsqrt(jnp.mean(centred * centred, -1, keepdims=True) + epsilon)


def nt_dot(a, b):
    return lax.dot_general(a, b, (((1,), (1,)), ((), ())), preferred_element_type=f32)


def start_copies(pairs, sems):
    copies = [pltpu.make_async_copy(a, b, sems.at[i]) for i, (a, b) in enumerate(pairs)]
    for copy in copies:
        copy.start()
    return copies


def project_kernel(
    single_hbm, weight_hbm, query_ref, kv_ref, single_ref, weight_ref, sems
):
    copies = start_copies(((single_hbm, single_ref), (weight_hbm, weight_ref)), sems)
    copies[0].wait()
    normed = normalize(single_ref[...].astype(f32)).astype(bf16)
    copies[1].wait()
    projected = nt_dot(weight_ref[...], normed)
    width = query_ref.shape[0] // 2
    query_ref[:width] = projected[:width].astype(bf16).astype(f32)
    query_ref[width:] = jax.nn.sigmoid(projected[3 * width :])
    kv_ref[...] = projected[width : 3 * width].astype(bf16)


def normalize_rows(rounded):
    values = rounded.astype(f32)
    width = values.shape[-1]
    centred = values - jnp.dot(
        rounded, jnp.full((width, width), 1.0 / width, bf16), preferred_element_type=f32
    )
    square = jnp.mean(centred * centred, -1, keepdims=True)
    return (centred * lax.rsqrt(square + epsilon)).astype(bf16)


def bias_kernel(
    pair_hbm,
    weight_hbm,
    mask_hbm,
    out_hbm,
    pair_ref,
    weight_ref,
    mask_ref,
    held_ref,
    staged_ref,
    sems,
    out_sems,
):
    tile_rows, tile_cols, width = pair_ref.shape
    targets, heads_there = staged_ref.shape[:2]
    pairs = heads_there // 2
    ends = [tile_rows // 4, 3 * tile_rows // 4, tile_rows]
    parts = [(weight_hbm, weight_ref), (mask_hbm.at[lax.axis_index("cols")], mask_ref)]
    at = 0
    for end in ends:
        rows_here = pl.ds(at, end - at)
        parts.append((pair_hbm.at[rows_here], pair_ref.at[rows_here]))
        at = end
    copies = start_copies(parts, sems)
    copies[0].wait()
    copies[1].wait()
    included = mask_ref[...] > 0
    at = 0
    outs = []
    for chunk, end in enumerate(ends):
        copies[2 + chunk].wait()
        step = end - at
        normed = normalize_rows(pair_ref[at:end].reshape(step * tile_cols, width))
        both = nt_dot(weight_ref[...], normed)
        for i in range(step):
            held_ref[:, i, :] = both[:, i * tile_cols : (i + 1) * tile_cols]
        held = jnp.where(included[None], held_ref[:, :step, :], lowest).astype(bf16)
        for d in range(targets):
            for p in range(heads_there // pairs):
                first = p * targets * pairs + d * pairs
                staged_ref[d, p * pairs : (p + 1) * pairs, at:end] = held[first : first + pairs]
        rows_here = pl.ds(at, step)
        out = pltpu.make_async_copy(
            staged_ref.at[:, :, rows_here], out_hbm.at[:, :, rows_here], out_sems.at[chunk]
        )
        out.start()
        outs.append(out)
        at = end
    for out in outs:
        out.wait()


def attend_kernel(
    own_ref, other_ref, bias_ref, near_ref, far_hbm, out_ref, score_ref, far_ref, sems
):
    copies = start_copies(((far_hbm, far_ref),), sems)
    blocks, heads_there, tile_rows, tile_cols = bias_ref.shape
    width = own_ref.shape[0] // 2
    pairs = heads_there // 2
    head_width = width // pairs
    score_scale = 1.0 / math.sqrt(head_width)
    shifts = near_ref.shape[0]
    row, col = lax.axis_index("rows"), lax.axis_index("cols")
    half, turn, core = row // (2 * shifts), (row // 2) % shifts, row % 2
    second = col // blocks

    def block(b, z, part):
        sent = (turn + shifts - b // 2) % shifts
        near, far = near_ref[sent, half ^ z, part, :], far_ref[sent, half ^ z, part, :]
        return jnp.where(core == b % 2, near, far)

    own, other = own_ref[...], other_ref[...]
    copies[0].wait()
    attended, gates, sums = [], [], []
    for z in range(2):
        here = jnp.where(second == z, own, other)
        query = jnp.transpose(here[:width]).astype(bf16)
        gates.append(here[width:])
        for h in range(pairs):
            query_head = query[:, h * head_width : (h + 1) * head_width]
            key_rows = pl.ds(h * head_width, head_width)
            value_rows = pl.ds(width + h * head_width, head_width)
            top = None
            for b in range(blocks):
                scores = jnp.dot(query_head, block(b, z, key_rows), preferred_element_type=f32)
                scores = scores * score_scale + bias_ref[b, z * pairs + h].astype(f32)
                score_ref[b] = scores
                top = scores if top is None else jnp.maximum(top, scores)
            top = jnp.max(top, axis=-1, keepdims=True)
            total = mixed = None
            for b in range(blocks):
                weights = jnp.exp(score_ref[b] - top)
                part = nt_dot(weights.astype(bf16), block(b, z, value_rows))
                total = weights if total is None else total + weights
                mixed = part if mixed is None else mixed + part
            total = jnp.sum(total, axis=-1, keepdims=True)
            attended.append(mixed / total)
            sums.append(top + jnp.log(total))
    def for_half(z, first, last):
        low = lax.broadcasted_iota(jnp.int32, first.shape, 1) < tile_rows // 2
        if z == 0:
            return jnp.where(low, first, pltpu.roll(last, tile_rows // 2, 1)).astype(bf16)
        return jnp.where(low, pltpu.roll(first, tile_rows // 2, 1), last).astype(bf16)

    gated = jnp.transpose(jnp.concatenate(attended, axis=1)) * jnp.concatenate(gates, axis=0)
    lane = lax.broadcasted_iota(jnp.int32, (tile_rows, 128), 1)
    coded_rows = out_ref.shape[1] - width
    coded = jnp.zeros((tile_rows, 128), f32)
    for h, value in enumerate(sums):
        for p in range(3):
            part = value.astype(bf16).astype(f32)
            value = value - part
            place = (h // pairs) * coded_rows + p * pairs + h % pairs
            coded = jnp.where(lane == place, part, coded)
    coded = jnp.transpose(coded)
    for z in range(2):
        values = for_half(z, gated[:width], gated[width:])
        codes = for_half(z, coded[:coded_rows], coded[coded_rows : 2 * coded_rows])
        for d in range(blocks):
            out_ref[z * blocks + d, :width] = values
            out_ref[z * blocks + d, width:] = codes


def factor_kernel(
    sent_ref,
    w_out_ref,
    single_hbm,
    w_factors_hbm,
    out_ref,
    factors_ref,
    joined_ref,
    single_ref,
    w_factors_ref,
    sems,
):
    blocks = sent_ref.shape[0] // 2
    width = joined_ref.shape[0] // blocks
    rows_here = out_ref.shape[0]
    mine = lax.axis_index("cols") // blocks
    copies = start_copies(
        (
            (single_hbm.at[pl.ds(mine * rows_here, rows_here)], single_ref),
            (w_factors_hbm, w_factors_ref),
        ),
        sems,
    )
    pairs = 2
    head_width = width // pairs

    def log_sum(d):
        coded = sent_ref[d, width:].astype(f32)
        parts = [coded[p * pairs : (p + 1) * pairs] for p in range(3)]
        return parts[0] + parts[1] + parts[2]

    for d in range(blocks):
        first, last = log_sum(d), log_sum(d + blocks)
        top = jnp.maximum(first, last)
        first, last = jnp.exp(first - top), jnp.exp(last - top)
        inverse = 1.0 / (first + last)
        first, last = first * inverse, last * inverse
        for h in range(pairs):
            here = pl.ds(h * head_width, head_width)
            joined = (
                sent_ref[d, here].astype(f32) * first[h : h + 1]
                + sent_ref[d + blocks, here].astype(f32) * last[h : h + 1]
            )
            place = d * width + h * head_width
            joined_ref[place : place + head_width] = joined.astype(bf16)
    mixed = jnp.transpose(joined_ref[...].astype(f32)).astype(bf16)
    depth = blocks * width
    head_total = jnp.dot(mixed[:rows_here], w_out_ref[:depth], preferred_element_type=f32)
    head_total += jnp.dot(mixed[rows_here:], w_out_ref[depth:], preferred_element_type=f32)
    copies[0].wait()
    single_out = (single_ref[...].astype(f32) + head_total).astype(bf16)
    out_ref[...] = single_out
    normed = normalize(single_out.astype(f32)).astype(bf16)
    copies[1].wait()
    factors_ref[...] = jnp.dot(normed, w_factors_ref[...], preferred_element_type=f32).astype(bf16)


def update_kernel(
    pair_ref,
    left_own_ref,
    left_other_ref,
    right_one_ref,
    right_two_ref,
    single_own_hbm,
    single_other_hbm,
    w_pairout_hbm,
    w_up_hbm,
    w_down_hbm,
    out_ref,
    single_hbm,
    w_pairout_ref,
    w_up_ref,
    w_down_ref,
    scale_ref,
    shift_ref,
    right_ref,
    sems,
):
    block_rows, tile_cols, width = pair_ref.shape
    factor_width = width // 2
    half = left_own_ref.shape[0]
    at = pl.program_id(0)
    col_half = lax.axis_index("cols") // (lax.axis_size("cols") // 2)
    row_half = lax.axis_index("rows") // (lax.axis_size("rows") // 2)
    copies = [
        pltpu.make_async_copy(w_pairout_hbm, w_pairout_ref, sems.at[0]),
        pltpu.make_async_copy(w_up_hbm, w_up_ref, sems.at[1]),
        pltpu.make_async_copy(w_down_hbm, w_down_ref, sems.at[2]),
    ]
    singles = [
        pltpu.make_async_copy(
            single_own_hbm, single_hbm.at[pl.ds(col_half * half, half)], sems.at[3]
        ),
        pltpu.make_async_copy(
            single_other_hbm, single_hbm.at[pl.ds((1 - col_half) * half, half)], sems.at[4]
        ),
    ]

    def in_order(first_is, one, two):
        top = jnp.where(first_is == 0, one, two)
        return jnp.concatenate([top, jnp.where(first_is == 0, two, one)], axis=0)

    @pl.when(at == 0)
    def _():
        for copy in copies + singles:
            copy.start()
        right = in_order(row_half, right_one_ref[...], right_two_ref[...])[:, factor_width:]
        right_ref[...] = jnp.concatenate([right, right], axis=1)
        left = in_order(col_half, left_own_ref[...], left_other_ref[...])[:, :factor_width]
        left = jnp.concatenate([left, left], axis=1).astype(f32)
        low = lax.broadcasted_iota(jnp.int32, (1, width), 1) < factor_width
        scale_ref[...] = jnp.where(low, left, -1.0).astype(bf16)[:, None, :]
        shift_ref[...] = jnp.where(low, 0.0, left).astype(bf16)[:, None, :]
        for copy in copies:
            copy.wait()

    rows_here = block_rows * tile_cols
    here = pl.ds(at * block_rows, block_rows)
    paired = (right_ref[...][None] * scale_ref[here] + shift_ref[here]).reshape(rows_here, width)
    moved = jnp.dot(paired, w_pairout_ref[...], preferred_element_type=f32)
    pair_mid = (pair_ref[...].reshape(rows_here, width).astype(f32) + moved).astype(bf16)
    normed = normalize_rows(pair_mid)
    hidden = jnp.dot(normed, w_up_ref[...], preferred_element_type=f32).astype(bf16)
    hidden = jnp.maximum(hidden, 0)
    down = jnp.dot(hidden, w_down_ref[...], preferred_element_type=f32)
    out_ref[...] = (pair_mid.astype(f32) + down).astype(bf16).reshape(pair_ref.shape)

    @pl.when(at == pl.num_programs(0) - 1)
    def _():
        for copy in singles:
            copy.wait()


def whole(shape):
    return pl.BlockSpec(shape, lambda *_: (0,) * len(shape))


def pinned(value):
    return pltpu.with_memory_space_constraint(value, pltpu.HBM)


def params(mib=8):
    return pltpu.CompilerParams(vmem_limit_bytes=mib * 1024 * 1024)


def per_device(
    single, pair, residue_mask, w_bias, w_project, w_out, w_factors, w_pairout, w_up, w_down
):
    tile_rows, tile_cols, pair_width = pair.shape
    single_width = single.shape[1]
    width = w_project.shape[2]
    rows, cols = lax.axis_size("rows"), lax.axis_size("cols")
    heads = w_bias.shape[1]
    in_place = pl.BlockSpec(memory_space=pl.ANY)
    in_hbm = pl.BlockSpec(memory_space=pltpu.HBM)
    in_vmem = pl.BlockSpec(memory_space=pltpu.VMEM)

    shifts = rows // 4
    half_rows, half_cols = rows // 2, cols // 2
    both_axes = ("rows", "cols")

    def sent(value, axes, target):
        if axes == "rows":
            routes = [(r, target(r)) for r in range(rows)]
        elif axes == "cols":
            routes = [(c, target(c)) for c in range(cols)]
        else:
            routes = []
            for r in range(rows):
                for c in range(cols):
                    to_row, to_col = target(r, c)
                    routes.append((r * cols + c, to_row * cols + to_col))
        return lax.ppermute(value, axes, routes)

    def rerouted(flip):
        def target(r, c):
            z_row, z_col = r // half_rows, c // half_cols
            return (z_col ^ flip) * half_rows + r % half_rows, z_row * half_cols + c % half_cols

        return target

    weight = jnp.transpose(w_project, (0, 2, 1)).reshape(4 * width, single_width)
    query, kv = pl.pallas_call(
        project_kernel,
        out_shape=(
            jax.ShapeDtypeStruct((2 * width, tile_rows), f32),
            jax.ShapeDtypeStruct((2 * width, tile_rows), bf16),
        ),
        in_specs=[in_hbm, in_hbm],
        scratch_shapes=[
            pltpu.VMEM(single.shape, bf16),
            pltpu.VMEM(weight.shape, bf16),
            pltpu.SemaphoreType.DMA((2,)),
        ],
        compiler_params=params(),
        name="project",
    )(pinned(single), pinned(weight))

    kv_first = sent(kv, both_axes, rerouted(0))
    kv_last = sent(kv, both_axes, rerouted(1))
    kv, w_bias = lax.optimization_barrier((kv, w_bias))

    heads_there = 2 * heads // cols
    sent_shape = (half_cols, heads_there, tile_rows, tile_cols)
    bias_local = pl.pallas_call(
        bias_kernel,
        out_shape=jax.ShapeDtypeStruct(sent_shape, bf16),
        in_specs=[in_hbm, in_hbm, in_hbm],
        out_specs=in_place,
        scratch_shapes=[
            pltpu.VMEM(pair.shape, bf16),
            pltpu.VMEM((heads, pair_width), bf16),
            pltpu.VMEM((1, tile_cols), jnp.int32),
            pltpu.VMEM((heads, tile_rows // 2, tile_cols), f32),
            pltpu.VMEM(sent_shape, bf16),
            pltpu.SemaphoreType.DMA((5,)),
            pltpu.SemaphoreType.DMA((3,)),
        ],
        compiler_params=params(28),
        name="bias",
    )(pinned(pair), pinned(jnp.transpose(w_bias)), pinned(residue_mask.reshape(cols, 1, tile_cols)))
    bias_local, kv_first, kv_last = lax.optimization_barrier((bias_local, kv_first, kv_last))
    groups = [list(range(half_cols)), list(range(half_cols, cols))]
    bias_heads = lax.all_to_all(bias_local, "cols", 0, 0, axis_index_groups=groups, tiled=True)

    query_other = sent(query, "cols", lambda c: c ^ half_cols)
    both = jnp.stack([kv_first, kv_last])
    near = [both]
    for s in range(1, shifts):
        around = lambda r: (r & half_rows) | ((r + 2 * s) & (half_rows - 1))
        near.append(sent(both, "rows", around))
    near = jnp.stack(near)
    far = sent(near, "rows", lambda r: r ^ 1)

    mixed = pl.pallas_call(
        attend_kernel,
        out_shape=jax.ShapeDtypeStruct((cols, width + 16, tile_rows), bf16),
        in_specs=[in_vmem] * 4 + [in_hbm],
        scratch_shapes=[
            pltpu.VMEM((half_cols, tile_rows, tile_cols), f32),
            pltpu.VMEM(near.shape, bf16),
            pltpu.SemaphoreType.DMA((1,)),
        ],
        compiler_params=params(),
        name="attend",
    )(query, query_other, bias_heads, near, pinned(far))
    mixed_all = lax.all_to_all(mixed, "cols", 0, 0, tiled=True)

    factor_shape = (tile_rows // 2, w_factors.shape[1])
    single_half, factors = pl.pallas_call(
        factor_kernel,
        out_shape=(
            jax.ShapeDtypeStruct((tile_rows // 2, single_width), bf16),
            jax.ShapeDtypeStruct(factor_shape, bf16),
        ),
        in_specs=[whole(mixed_all.shape), whole(w_out.shape), in_hbm, in_hbm],
        scratch_shapes=[
            pltpu.VMEM((single_width // 2, tile_rows), bf16),
            pltpu.VMEM((tile_rows // 2, single_width), bf16),
            pltpu.VMEM(w_factors.shape, bf16),
            pltpu.SemaphoreType.DMA((2,)),
        ],
        compiler_params=params(),
        name="factor",
    )(mixed_all, w_out, pinned(single), pinned(w_factors))

    right_one = sent(factors, both_axes, lambda r, c: (c, r))
    right_two = sent(factors, both_axes, lambda r, c: (c ^ half_rows, r))
    left_other = sent(factors, "cols", lambda c: c ^ half_cols)
    single_other = sent(single_half, "cols", lambda c: c ^ half_cols)

    block_rows = 32
    pair_block = pl.BlockSpec((block_rows, tile_cols, pair_width), lambda i: (i, 0, 0))
    updated, single_out = pl.pallas_call(
        update_kernel,
        grid=(tile_rows // block_rows,),
        in_specs=[pair_block] + [whole(factor_shape)] * 4 + [in_place] * 2 + [in_hbm] * 3,
        out_specs=(pair_block, in_place),
        out_shape=(
            jax.ShapeDtypeStruct(pair.shape, bf16),
            jax.ShapeDtypeStruct(single.shape, bf16),
        ),
        scratch_shapes=[
            pltpu.VMEM(w_pairout.shape, bf16),
            pltpu.VMEM(w_up.shape, bf16),
            pltpu.VMEM(w_down.shape, bf16),
            pltpu.VMEM((tile_rows, 1, pair_width), bf16),
            pltpu.VMEM((tile_rows, 1, pair_width), bf16),
            pltpu.VMEM((tile_cols, pair_width), bf16),
            pltpu.SemaphoreType.DMA((5,)),
        ],
        compiler_params=params(20),
        name="update",
    )(
        pair,
        factors,
        left_other,
        right_one,
        right_two,
        single_half,
        single_other,
        pinned(w_pairout),
        pinned(w_up),
        pinned(w_down),
    )
    return (single_out, updated)


def solution(mesh):
    return jax.shard_map(
        per_device,
        mesh=mesh,
        in_specs=(
            P("rows", None),
            P("rows", "cols", None),
            P(),
            P(),
            P(None, None, "cols"),
            P(),
            P(),
            P(),
            P(),
            P(),
        ),
        out_specs=(P("rows", None), P("rows", "cols", None)),
        check_vma=False,
    )
```

```python
import functools
import math

import jax
import jax.numpy as jnp
from jax import lax
from jax.experimental import pallas as pl
from jax.experimental.pallas import tpu as pltpu
from jax.sharding import PartitionSpec as P

epsilon = 1e-05
f32 = jnp.float32
bf16 = jnp.bfloat16
lowest = -1e30


def normalize(values):
    centred = values - jnp.mean(values, -1, keepdims=True)
    return centred * lax.rsqrt(jnp.mean(centred * centred, -1, keepdims=True) + epsilon)


def nt_dot(a, b):
    return lax.dot_general(a, b, (((1,), (1,)), ((), ())), preferred_element_type=f32)


def start_copies(pairs, sems):
    copies = [pltpu.make_async_copy(a, b, sems.at[i]) for i, (a, b) in enumerate(pairs)]
    for copy in copies:
        copy.start()
    return copies


def project_kernel(
    single_hbm, weight_hbm, query_ref, kv_ref, single_ref, weight_ref, sems
):
    copies = start_copies(((single_hbm, single_ref), (weight_hbm, weight_ref)), sems)
    copies[0].wait()
    normed = normalize(single_ref[...].astype(f32)).astype(bf16)
    copies[1].wait()
    projected = nt_dot(weight_ref[...], normed)
    width = query_ref.shape[0] // 2
    query_ref[:width] = projected[:width].astype(bf16).astype(f32)
    query_ref[width:] = jax.nn.sigmoid(projected[3 * width :])
    kv_ref[...] = projected[width : 3 * width].astype(bf16)


def normalize_rows(rounded):
    values = rounded.astype(f32)
    width = values.shape[-1]
    centred = values - jnp.dot(
        rounded, jnp.full((width, width), 1.0 / width, bf16), preferred_element_type=f32
    )
    square = jnp.mean(centred * centred, -1, keepdims=True)
    return (centred * lax.rsqrt(square + epsilon)).astype(bf16)


def bias_kernel(
    pair_hbm,
    weight_hbm,
    mask_hbm,
    out_hbm,
    pair_ref,
    weight_ref,
    mask_ref,
    held_ref,
    staged_ref,
    sems,
    out_sems,
):
    tile_rows, tile_cols, width = pair_ref.shape
    targets, heads_there = staged_ref.shape[:2]
    pairs = heads_there // 2
    ends = [tile_rows // 4, 3 * tile_rows // 4, tile_rows]
    parts = [(weight_hbm, weight_ref), (mask_hbm.at[lax.axis_index("cols")], mask_ref)]
    at = 0
    for end in ends:
        rows_here = pl.ds(at, end - at)
        parts.append((pair_hbm.at[rows_here], pair_ref.at[rows_here]))
        at = end
    copies = start_copies(parts, sems)
    copies[0].wait()
    copies[1].wait()
    included = mask_ref[...] > 0
    at = 0
    outs = []
    for chunk, end in enumerate(ends):
        copies[2 + chunk].wait()
        step = end - at
        normed = normalize_rows(pair_ref[at:end].reshape(step * tile_cols, width))
        both = nt_dot(weight_ref[...], normed)
        for i in range(step):
            held_ref[:, i, :] = both[:, i * tile_cols : (i + 1) * tile_cols]
        held = jnp.where(included[None], held_ref[:, :step, :], lowest).astype(bf16)
        for d in range(targets):
            for p in range(heads_there // pairs):
                first = p * targets * pairs + d * pairs
                staged_ref[d, p * pairs : (p + 1) * pairs, at:end] = held[first : first + pairs]
        rows_here = pl.ds(at, step)
        out = pltpu.make_async_copy(
            staged_ref.at[:, :, rows_here], out_hbm.at[:, :, rows_here], out_sems.at[chunk]
        )
        out.start()
        outs.append(out)
        at = end
    for out in outs:
        out.wait()


def attend_kernel(
    own_hbm,
    other_hbm,
    bias_ref,
    near_ref,
    far_hbm,
    kept_ref,
    sent_ref,
    score_ref,
    own_ref,
    other_ref,
    far_ref,
    sems,
):
    copies = start_copies(
        ((own_hbm, own_ref), (other_hbm, other_ref), (far_hbm, far_ref)), sems
    )
    blocks, heads_there, tile_rows, tile_cols = bias_ref.shape
    width = own_ref.shape[0] // 2
    pairs = heads_there // 2
    head_width = width // pairs
    score_scale = 1.0 / math.sqrt(head_width)
    shifts = near_ref.shape[0]
    row, col = lax.axis_index("rows"), lax.axis_index("cols")
    half, turn, core = row // (2 * shifts), (row // 2) % shifts, row % 2
    second = col // blocks

    def block(b, z, part):
        sent = (turn + shifts - b // 2) % shifts
        near, far = near_ref[sent, half ^ z, part, :], far_ref[sent, half ^ z, part, :]
        return jnp.where(core == b % 2, near, far)

    for copy in copies:
        copy.wait()
    lane = lax.broadcasted_iota(jnp.int32, (tile_rows, 128), 1)
    for slot, query_ref in enumerate((own_ref, other_ref)):
        z = second ^ slot
        query = jnp.transpose(query_ref[:width]).astype(bf16)
        attended, sums = [], []
        for h in range(pairs):
            query_head = query[:, h * head_width : (h + 1) * head_width]
            key_rows = pl.ds(h * head_width, head_width)
            value_rows = pl.ds(width + h * head_width, head_width)
            top = None
            for b in range(blocks):
                scores = jnp.dot(query_head, block(b, z, key_rows), preferred_element_type=f32)
                scores = scores * score_scale + bias_ref[b, z * pairs + h].astype(f32)
                score_ref[b] = scores
                top = scores if top is None else jnp.maximum(top, scores)
            top = jnp.max(top, axis=-1, keepdims=True)
            total = mixed = None
            for b in range(blocks):
                weights = jnp.exp(score_ref[b] - top)
                part = nt_dot(weights.astype(bf16), block(b, z, value_rows))
                total = weights if total is None else total + weights
                mixed = part if mixed is None else mixed + part
            total = jnp.sum(total, axis=-1, keepdims=True)
            attended.append(mixed / total)
            sums.append(top + jnp.log(total))
        gated = jnp.transpose(jnp.concatenate(attended, axis=1)) * query_ref[width:]
        coded = jnp.zeros((tile_rows, 128), f32)
        for h, value in enumerate(sums):
            if slot == 0:
                coded = jnp.where(lane == h, value, coded)
                continue
            for p in range(3):
                part = value.astype(bf16).astype(f32)
                value = value - part
                coded = jnp.where(lane == p * pairs + h, part, coded)
        out_ref = sent_ref if slot else kept_ref
        out_ref[:width] = gated.astype(out_ref.dtype)
        out_ref[width:] = jnp.transpose(coded)[: out_ref.shape[0] - width].astype(out_ref.dtype)


def join_kernel(kept_ref, received_ref, out_ref):
    width = out_ref.shape[1]
    pairs = 2
    head_width = width // pairs
    first = kept_ref[width : width + pairs]
    coded = received_ref[width:].astype(f32)
    last = coded[:pairs] + coded[pairs : 2 * pairs] + coded[2 * pairs : 3 * pairs]
    top = jnp.maximum(first, last)
    first, last = jnp.exp(first - top), jnp.exp(last - top)
    inverse = 1.0 / (first + last)
    first, last = first * inverse, last * inverse
    for h in range(pairs):
        here = pl.ds(h * head_width, head_width)
        joined = kept_ref[here] * first[h : h + 1]
        joined += received_ref[here].astype(f32) * last[h : h + 1]
        for d in range(out_ref.shape[0]):
            out_ref[d, here] = joined.astype(bf16)


def factor_kernel(
    mixed_ref,
    w_out_ref,
    single_hbm,
    w_factors_hbm,
    out_ref,
    factors_ref,
    single_ref,
    w_factors_ref,
    sems,
):
    copies = start_copies(((single_hbm, single_ref), (w_factors_hbm, w_factors_ref)), sems)
    mixed = jnp.transpose(mixed_ref[...].astype(f32)).astype(bf16)
    head_total = jnp.dot(mixed, w_out_ref[...], preferred_element_type=f32)
    copies[0].wait()
    single_out = (single_ref[...].astype(f32) + head_total).astype(bf16)
    out_ref[...] = single_out
    normed = normalize(single_out.astype(f32)).astype(bf16)
    copies[1].wait()
    factors_ref[...] = jnp.dot(normed, w_factors_ref[...], preferred_element_type=f32).astype(bf16)


def update_kernel(
    pair_ref,
    left_ref,
    right_factors_ref,
    w_pairout_hbm,
    w_up_hbm,
    w_down_hbm,
    out_ref,
    w_pairout_ref,
    w_up_ref,
    w_down_ref,
    scale_ref,
    shift_ref,
    right_ref,
    sems,
):
    block_rows, tile_cols, width = pair_ref.shape
    factor_width = width // 2
    at = pl.program_id(0)

    @pl.when(at == 0)
    def _():
        copies = start_copies(
            (
                (w_pairout_hbm, w_pairout_ref),
                (w_up_hbm, w_up_ref),
                (w_down_hbm, w_down_ref),
            ),
            sems,
        )
        right = right_factors_ref[:, factor_width:]
        right_ref[...] = jnp.concatenate([right, right], axis=1)
        left = left_ref[:, :factor_width].astype(f32)
        left = jnp.concatenate([left, left], axis=1)
        low = lax.broadcasted_iota(jnp.int32, (1, width), 1) < factor_width
        scale_ref[...] = jnp.where(low, left, -1.0).astype(bf16)[:, None, :]
        shift_ref[...] = jnp.where(low, 0.0, left).astype(bf16)[:, None, :]
        for copy in copies:
            copy.wait()

    rows_here = block_rows * tile_cols
    here = pl.ds(at * block_rows, block_rows)
    paired = (right_ref[...][None] * scale_ref[here] + shift_ref[here]).reshape(rows_here, width)
    moved = jnp.dot(paired, w_pairout_ref[...], preferred_element_type=f32)
    pair_mid = (pair_ref[...].reshape(rows_here, width).astype(f32) + moved).astype(bf16)
    normed = normalize_rows(pair_mid)
    hidden = jnp.dot(normed, w_up_ref[...], preferred_element_type=f32).astype(bf16)
    hidden = jnp.maximum(hidden, 0)
    down = jnp.dot(hidden, w_down_ref[...], preferred_element_type=f32)
    out_ref[...] = (pair_mid.astype(f32) + down).astype(bf16).reshape(pair_ref.shape)


def whole(shape):
    return pl.BlockSpec(shape, lambda *_: (0,) * len(shape))


def pinned(value):
    return pltpu.with_memory_space_constraint(value, pltpu.HBM)


def params(mib=8):
    return pltpu.CompilerParams(vmem_limit_bytes=mib * 1024 * 1024)


def per_device(
    single, pair, residue_mask, w_bias, w_project, w_out, w_factors, w_pairout, w_up, w_down
):
    tile_rows, tile_cols, pair_width = pair.shape
    single_width = single.shape[1]
    width = w_project.shape[2]
    rows, cols = lax.axis_size("rows"), lax.axis_size("cols")
    heads = w_bias.shape[1]
    in_place = pl.BlockSpec(memory_space=pl.ANY)
    in_hbm = pl.BlockSpec(memory_space=pltpu.HBM)
    in_vmem = pl.BlockSpec(memory_space=pltpu.VMEM)

    shifts = rows // 4
    half_rows, half_cols = rows // 2, cols // 2
    both_axes = ("rows", "cols")

    def sent(value, axes, target):
        if axes == "rows":
            routes = [(r, target(r)) for r in range(rows)]
        elif axes == "cols":
            routes = [(c, target(c)) for c in range(cols)]
        else:
            routes = []
            for r in range(rows):
                for c in range(cols):
                    to_row, to_col = target(r, c)
                    routes.append((r * cols + c, to_row * cols + to_col))
        return lax.ppermute(value, axes, routes)

    def rerouted(flip):
        def target(r, c):
            z_row, z_col = r // half_rows, c // half_cols
            return (z_col ^ flip) * half_rows + r % half_rows, z_row * half_cols + c % half_cols

        return target

    weight = jnp.transpose(w_project, (0, 2, 1)).reshape(4 * width, single_width)
    query, kv = pl.pallas_call(
        project_kernel,
        out_shape=(
            jax.ShapeDtypeStruct((2 * width, tile_rows), f32),
            jax.ShapeDtypeStruct((2 * width, tile_rows), bf16),
        ),
        in_specs=[in_hbm, in_hbm],
        scratch_shapes=[
            pltpu.VMEM(single.shape, bf16),
            pltpu.VMEM(weight.shape, bf16),
            pltpu.SemaphoreType.DMA((2,)),
        ],
        compiler_params=params(),
        name="project",
    )(pinned(single), pinned(weight))

    kv_first = sent(kv, both_axes, rerouted(0))
    kv_last = sent(kv, both_axes, rerouted(1))
    kv, w_bias = lax.optimization_barrier((kv, w_bias))

    heads_there = 2 * heads // cols
    sent_shape = (half_cols, heads_there, tile_rows, tile_cols)
    bias_local = pl.pallas_call(
        bias_kernel,
        out_shape=jax.ShapeDtypeStruct(sent_shape, bf16),
        in_specs=[in_hbm, in_hbm, in_hbm],
        out_specs=in_place,
        scratch_shapes=[
            pltpu.VMEM(pair.shape, bf16),
            pltpu.VMEM((heads, pair_width), bf16),
            pltpu.VMEM((1, tile_cols), jnp.int32),
            pltpu.VMEM((heads, tile_rows // 2, tile_cols), f32),
            pltpu.VMEM(sent_shape, bf16),
            pltpu.SemaphoreType.DMA((5,)),
            pltpu.SemaphoreType.DMA((3,)),
        ],
        compiler_params=params(28),
        name="bias",
    )(pinned(pair), pinned(jnp.transpose(w_bias)), pinned(residue_mask.reshape(cols, 1, tile_cols)))
    query_other = sent(query, "cols", lambda c: c ^ half_cols)
    bias_local, kv_first, kv_last, query_other = lax.optimization_barrier(
        (bias_local, kv_first, kv_last, query_other)
    )
    groups = [list(range(half_cols)), list(range(half_cols, cols))]
    bias_heads = lax.all_to_all(bias_local, "cols", 0, 0, axis_index_groups=groups, tiled=True)

    both = jnp.stack([kv_first, kv_last])
    near = [both]
    for s in range(1, shifts):
        around = lambda r: (r & half_rows) | ((r + 2 * s) & (half_rows - 1))
        near.append(sent(both, "rows", around))
    near = jnp.stack(near)
    far = sent(near, "rows", lambda r: r ^ 1)

    kept, partial = pl.pallas_call(
        attend_kernel,
        out_shape=(
            jax.ShapeDtypeStruct((width + 8, tile_rows), f32),
            jax.ShapeDtypeStruct((width + 16, tile_rows), bf16),
        ),
        in_specs=[in_hbm, in_hbm, in_vmem, in_vmem, in_hbm],
        scratch_shapes=[
            pltpu.VMEM((half_cols, tile_rows, tile_cols), f32),
            pltpu.VMEM(query.shape, f32),
            pltpu.VMEM(query.shape, f32),
            pltpu.VMEM(near.shape, bf16),
            pltpu.SemaphoreType.DMA((3,)),
        ],
        compiler_params=params(),
        name="attend",
    )(pinned(query), pinned(query_other), bias_heads, near, pinned(far))
    received = sent(partial, "cols", lambda c: c ^ half_cols)
    mixed = pl.pallas_call(
        join_kernel,
        out_shape=jax.ShapeDtypeStruct((cols, width, tile_rows), bf16),
        compiler_params=params(),
        name="join",
    )(kept, received)
    mixed_all = lax.all_to_all(mixed, "cols", 0, 0, tiled=True).reshape(single_width, tile_rows)

    single_out, factors = pl.pallas_call(
        factor_kernel,
        out_shape=(
            jax.ShapeDtypeStruct(single.shape, bf16),
            jax.ShapeDtypeStruct((tile_rows, w_factors.shape[1]), bf16),
        ),
        in_specs=[whole(mixed_all.shape), whole(w_out.shape), in_hbm, in_hbm],
        scratch_shapes=[
            pltpu.VMEM(single.shape, bf16),
            pltpu.VMEM(w_factors.shape, bf16),
            pltpu.SemaphoreType.DMA((2,)),
        ],
        compiler_params=params(),
        name="factor",
    )(mixed_all, w_out, pinned(single), pinned(w_factors))

    right_factors = sent(factors, both_axes, lambda r, c: (c, r))

    block_rows = 32
    pair_block = pl.BlockSpec((block_rows, tile_cols, pair_width), lambda i: (i, 0, 0))
    updated = pl.pallas_call(
        update_kernel,
        grid=(tile_rows // block_rows,),
        in_specs=[pair_block] + [whole(factors.shape)] * 2 + [in_place] * 3,
        out_specs=pair_block,
        out_shape=jax.ShapeDtypeStruct(pair.shape, bf16),
        scratch_shapes=[
            pltpu.VMEM(w_pairout.shape, bf16),
            pltpu.VMEM(w_up.shape, bf16),
            pltpu.VMEM(w_down.shape, bf16),
            pltpu.VMEM((tile_rows, 1, pair_width), bf16),
            pltpu.VMEM((tile_rows, 1, pair_width), bf16),
            pltpu.VMEM((tile_cols, pair_width), bf16),
            pltpu.SemaphoreType.DMA((3,)),
        ],
        compiler_params=params(20),
        name="update",
    )(pair, factors, right_factors, w_pairout, w_up, w_down)
    return (single_out, updated)


def solution(mesh):
    return jax.shard_map(
        per_device,
        mesh=mesh,
        in_specs=(
            P("rows", None),
            P("rows", "cols", None),
            P(),
            P(),
            P(None, None, "cols"),
            P(),
            P(),
            P(),
            P(),
            P(),
        ),
        out_specs=(P("rows", None), P("rows", "cols", None)),
        check_vma=False,
    )
```

```python
import functools
import math

import jax
import jax.numpy as jnp
from jax import lax
from jax.experimental import pallas as pl
from jax.experimental.pallas import tpu as pltpu
from jax.sharding import PartitionSpec as P

epsilon = 1e-05
f32 = jnp.float32
bf16 = jnp.bfloat16
lowest = -1e30


def normalize(values):
    centred = values - jnp.mean(values, -1, keepdims=True)
    return centred * lax.rsqrt(jnp.mean(centred * centred, -1, keepdims=True) + epsilon)


def nt_dot(a, b):
    return lax.dot_general(a, b, (((1,), (1,)), ((), ())), preferred_element_type=f32)


def start_copies(pairs, sems):
    copies = [pltpu.make_async_copy(a, b, sems.at[i]) for i, (a, b) in enumerate(pairs)]
    for copy in copies:
        copy.start()
    return copies


def project_kernel(
    single_hbm, weight_hbm, query_ref, kv_ref, single_ref, weight_ref, sems
):
    copies = start_copies(((single_hbm, single_ref), (weight_hbm, weight_ref)), sems)
    copies[0].wait()
    normed = normalize(single_ref[...].astype(f32)).astype(bf16)
    copies[1].wait()
    projected = nt_dot(weight_ref[...], normed)
    width = query_ref.shape[0] // 2
    query_ref[:width] = projected[:width].astype(bf16).astype(f32)
    query_ref[width:] = jax.nn.sigmoid(projected[3 * width :])
    kv_ref[...] = projected[width : 3 * width].astype(bf16)


def normalize_rows(rounded):
    values = rounded.astype(f32)
    width = values.shape[-1]
    centred = values - jnp.dot(
        rounded, jnp.full((width, width), 1.0 / width, bf16), preferred_element_type=f32
    )
    square = jnp.mean(centred * centred, -1, keepdims=True)
    return (centred * lax.rsqrt(square + epsilon)).astype(bf16)


def bias_kernel(
    pair_hbm,
    weight_hbm,
    mask_hbm,
    out_hbm,
    pair_ref,
    weight_ref,
    mask_ref,
    held_ref,
    staged_ref,
    sems,
    out_sems,
):
    tile_rows, tile_cols, width = pair_ref.shape
    targets, heads_there = staged_ref.shape[:2]
    pairs = heads_there // 2
    ends = [tile_rows // 4, tile_rows]
    parts = [(weight_hbm, weight_ref), (mask_hbm.at[lax.axis_index("cols")], mask_ref)]
    at = 0
    for end in ends:
        rows_here = pl.ds(at, end - at)
        parts.append((pair_hbm.at[rows_here], pair_ref.at[rows_here]))
        at = end
    copies = start_copies(parts, sems)
    copies[0].wait()
    copies[1].wait()
    included = mask_ref[...] > 0
    at = 0
    outs = []
    for chunk, end in enumerate(ends):
        copies[2 + chunk].wait()
        step = end - at
        normed = normalize_rows(pair_ref[at:end].reshape(step * tile_cols, width))
        both = nt_dot(weight_ref[...], normed)
        for i in range(step):
            held_ref[:, i, :] = both[:, i * tile_cols : (i + 1) * tile_cols]
        held = jnp.where(included[None], held_ref[:, :step, :], lowest).astype(bf16)
        for d in range(targets):
            for p in range(heads_there // pairs):
                first = p * targets * pairs + d * pairs
                staged_ref[d, p * pairs : (p + 1) * pairs, at:end] = held[first : first + pairs]
        rows_here = pl.ds(at, step)
        out = pltpu.make_async_copy(
            staged_ref.at[:, :, rows_here], out_hbm.at[:, :, rows_here], out_sems.at[chunk]
        )
        out.start()
        outs.append(out)
        at = end
    for out in outs:
        out.wait()


def attend_kernel(
    own_hbm,
    other_hbm,
    bias_ref,
    near_ref,
    far_hbm,
    single_hbm,
    w_factors_hbm,
    kept_ref,
    sent_ref,
    single_ref,
    w_factors_ref,
    score_ref,
    own_ref,
    other_ref,
    far_ref,
    sems,
):
    copies = start_copies(
        (
            (own_hbm, own_ref),
            (other_hbm, other_ref),
            (far_hbm, far_ref),
            (single_hbm, single_ref),
            (w_factors_hbm, w_factors_ref),
        ),
        sems,
    )
    blocks, heads_there, tile_rows, tile_cols = bias_ref.shape
    width = own_ref.shape[0] // 2
    pairs = heads_there // 2
    head_width = width // pairs
    score_scale = 1.0 / math.sqrt(head_width)
    shifts = near_ref.shape[0]
    row, col = lax.axis_index("rows"), lax.axis_index("cols")
    half, turn, core = row // (2 * shifts), (row // 2) % shifts, row % 2
    second = col // blocks

    def block(b, z, part):
        sent = (turn + shifts - b // 2) % shifts
        near, far = near_ref[sent, half ^ z, part, :], far_ref[sent, half ^ z, part, :]
        return jnp.where(core == b % 2, near, far)

    for copy in copies[:3]:
        copy.wait()
    lane = lax.broadcasted_iota(jnp.int32, (tile_rows, 128), 1)
    for slot, query_ref in enumerate((own_ref, other_ref)):
        z = second ^ slot
        query = jnp.transpose(query_ref[:width]).astype(bf16)
        attended, sums = [], []
        for h in range(pairs):
            query_head = query[:, h * head_width : (h + 1) * head_width]
            key_rows = pl.ds(h * head_width, head_width)
            value_rows = pl.ds(width + h * head_width, head_width)
            top = None
            for b in range(blocks):
                scores = jnp.dot(query_head, block(b, z, key_rows), preferred_element_type=f32)
                scores = scores * score_scale + bias_ref[b, z * pairs + h].astype(f32)
                score_ref[b] = scores
                top = scores if top is None else jnp.maximum(top, scores)
            top = jnp.max(top, axis=-1, keepdims=True)
            total = mixed = None
            for b in range(blocks):
                weights = jnp.exp(score_ref[b] - top)
                part = nt_dot(weights.astype(bf16), block(b, z, value_rows))
                total = weights if total is None else total + weights
                mixed = part if mixed is None else mixed + part
            total = jnp.sum(total, axis=-1, keepdims=True)
            attended.append(mixed / total)
            sums.append(top + jnp.log(total))
        gated = jnp.transpose(jnp.concatenate(attended, axis=1)) * query_ref[width:]
        coded = jnp.zeros((tile_rows, 128), f32)
        for h, value in enumerate(sums):
            if slot == 0:
                coded = jnp.where(lane == h, value, coded)
                continue
            for p in range(3):
                part = value.astype(bf16).astype(f32)
                value = value - part
                coded = jnp.where(lane == p * pairs + h, part, coded)
        out_ref = sent_ref if slot else kept_ref
        out_ref[:width] = gated.astype(out_ref.dtype)
        out_ref[width:] = jnp.transpose(coded)[: out_ref.shape[0] - width].astype(out_ref.dtype)
    for copy in copies[3:]:
        copy.wait()


def join_kernel(kept_ref, received_ref, out_ref):
    width = out_ref.shape[1]
    pairs = 2
    head_width = width // pairs
    first = kept_ref[width : width + pairs]
    coded = received_ref[width:].astype(f32)
    last = coded[:pairs] + coded[pairs : 2 * pairs] + coded[2 * pairs : 3 * pairs]
    top = jnp.maximum(first, last)
    first, last = jnp.exp(first - top), jnp.exp(last - top)
    inverse = 1.0 / (first + last)
    first, last = first * inverse, last * inverse
    for h in range(pairs):
        here = pl.ds(h * head_width, head_width)
        joined = kept_ref[here] * first[h : h + 1]
        joined += received_ref[here].astype(f32) * last[h : h + 1]
        for d in range(out_ref.shape[0]):
            out_ref[d, here] = joined.astype(bf16)


def factor_kernel(
    mixed_ref,
    w_out_ref,
    single_ref,
    w_factors_ref,
    w_pairout_hbm,
    w_up_hbm,
    w_down_hbm,
    out_ref,
    factors_ref,
    w_pairout_ref,
    w_up_ref,
    w_down_ref,
    sems,
):
    copies = start_copies(
        ((w_pairout_hbm, w_pairout_ref), (w_up_hbm, w_up_ref), (w_down_hbm, w_down_ref)), sems
    )
    mixed = jnp.transpose(mixed_ref[...].astype(f32)).astype(bf16)
    head_total = jnp.dot(mixed, w_out_ref[...], preferred_element_type=f32)
    single_out = (single_ref[...].astype(f32) + head_total).astype(bf16)
    out_ref[...] = single_out
    normed = normalize(single_out.astype(f32)).astype(bf16)
    factors_ref[...] = jnp.dot(normed, w_factors_ref[...], preferred_element_type=f32).astype(bf16)
    for copy in copies:
        copy.wait()


def update_kernel(
    pair_ref,
    left_ref,
    right_factors_ref,
    w_pairout_ref,
    w_up_ref,
    w_down_ref,
    out_ref,
    scale_ref,
    shift_ref,
    right_ref,
):
    block_rows, tile_cols, width = pair_ref.shape
    factor_width = width // 2
    at = pl.program_id(0)

    @pl.when(at == 0)
    def _():
        right = right_factors_ref[:, factor_width:]
        right_ref[...] = jnp.concatenate([right, right], axis=1)
        left = left_ref[:, :factor_width].astype(f32)
        left = jnp.concatenate([left, left], axis=1)
        low = lax.broadcasted_iota(jnp.int32, (1, width), 1) < factor_width
        scale_ref[...] = jnp.where(low, left, -1.0).astype(bf16)[:, None, :]
        shift_ref[...] = jnp.where(low, 0.0, left).astype(bf16)[:, None, :]

    rows_here = block_rows * tile_cols
    here = pl.ds(at * block_rows, block_rows)
    paired = (right_ref[...][None] * scale_ref[here] + shift_ref[here]).reshape(rows_here, width)
    moved = jnp.dot(paired, w_pairout_ref[...], preferred_element_type=f32)
    pair_mid = (pair_ref[...].reshape(rows_here, width).astype(f32) + moved).astype(bf16)
    normed = normalize_rows(pair_mid)
    hidden = jnp.dot(normed, w_up_ref[...], preferred_element_type=f32).astype(bf16)
    hidden = jnp.maximum(hidden, 0)
    down = jnp.dot(hidden, w_down_ref[...], preferred_element_type=f32)
    out_ref[...] = (pair_mid.astype(f32) + down).astype(bf16).reshape(pair_ref.shape)


def nearest_rows(row, count):
    def ring(a, b, length):
        apart = abs(a - b) % length
        return min(apart, length - apart)

    def cost(col, target):
        z = (row // 8) * 4 + col // 4, (target // 8) * 4 + row // 4
        y = (row // 2) % 4, (target // 2) % 4
        apart = ring(*z, 8) + ring(*y, 4) + ring(col % 4, row % 4, 4) + 0.3 * (row % 2 != target % 2)
        return apart**4

    chosen = list(range(count))
    better = True
    while better:
        better = False
        for a in range(count):
            for b in range(a):
                now = cost(a, chosen[a]) + cost(b, chosen[b])
                if cost(a, chosen[b]) + cost(b, chosen[a]) < now - 1e-9:
                    chosen[a], chosen[b] = chosen[b], chosen[a]
                    better = True
    return chosen


def whole(shape):
    return pl.BlockSpec(shape, lambda *_: (0,) * len(shape))


def pinned(value):
    return pltpu.with_memory_space_constraint(value, pltpu.HBM)


def params(mib=8):
    return pltpu.CompilerParams(vmem_limit_bytes=mib * 1024 * 1024)


def per_device(
    single, pair, residue_mask, w_bias, w_project, w_out, w_factors, w_pairout, w_up, w_down
):
    tile_rows, tile_cols, pair_width = pair.shape
    single_width = single.shape[1]
    width = w_project.shape[2]
    rows, cols = lax.axis_size("rows"), lax.axis_size("cols")
    heads = w_bias.shape[1]
    in_place = pl.BlockSpec(memory_space=pl.ANY)
    in_hbm = pl.BlockSpec(memory_space=pltpu.HBM)
    in_vmem = pl.BlockSpec(memory_space=pltpu.VMEM)

    shifts = rows // 4
    half_rows, half_cols = rows // 2, cols // 2
    both_axes = ("rows", "cols")

    def sent(value, axes, target):
        if axes == "rows":
            routes = [(r, target(r)) for r in range(rows)]
        elif axes == "cols":
            routes = [(c, target(c)) for c in range(cols)]
        else:
            routes = []
            for r in range(rows):
                for c in range(cols):
                    to_row, to_col = target(r, c)
                    routes.append((r * cols + c, to_row * cols + to_col))
        return lax.ppermute(value, axes, routes)

    def rerouted(flip):
        def target(r, c):
            z_row, z_col = r // half_rows, c // half_cols
            return (z_col ^ flip) * half_rows + r % half_rows, z_row * half_cols + c % half_cols

        return target

    weight = jnp.transpose(w_project, (0, 2, 1)).reshape(4 * width, single_width)
    query, kv = pl.pallas_call(
        project_kernel,
        out_shape=(
            jax.ShapeDtypeStruct((2 * width, tile_rows), f32),
            jax.ShapeDtypeStruct((2 * width, tile_rows), bf16),
        ),
        in_specs=[in_hbm, in_hbm],
        scratch_shapes=[
            pltpu.VMEM(single.shape, bf16),
            pltpu.VMEM(weight.shape, bf16),
            pltpu.SemaphoreType.DMA((2,)),
        ],
        compiler_params=params(),
        name="project",
    )(pinned(single), pinned(weight))

    kv_first = sent(kv, both_axes, rerouted(0))
    kv_last = sent(kv, both_axes, rerouted(1))
    kv, w_bias = lax.optimization_barrier((kv, w_bias))

    heads_there = 2 * heads // cols
    sent_shape = (half_cols, heads_there, tile_rows, tile_cols)
    bias_local = pl.pallas_call(
        bias_kernel,
        out_shape=jax.ShapeDtypeStruct(sent_shape, bf16),
        in_specs=[in_hbm, in_hbm, in_hbm],
        out_specs=in_place,
        scratch_shapes=[
            pltpu.VMEM(pair.shape, bf16),
            pltpu.VMEM((heads, pair_width), bf16),
            pltpu.VMEM((1, tile_cols), jnp.int32),
            pltpu.VMEM((heads, 3 * tile_rows // 4, tile_cols), f32),
            pltpu.VMEM(sent_shape, bf16),
            pltpu.SemaphoreType.DMA((4,)),
            pltpu.SemaphoreType.DMA((2,)),
        ],
        compiler_params=params(28),
        name="bias",
    )(pinned(pair), pinned(jnp.transpose(w_bias)), pinned(residue_mask.reshape(cols, 1, tile_cols)))
    query_other = sent(query, "cols", lambda c: c ^ half_cols)
    bias_local, kv_first, kv_last = lax.optimization_barrier((bias_local, kv_first, kv_last))
    groups = [list(range(half_cols)), list(range(half_cols, cols))]
    bias_heads = lax.all_to_all(bias_local, "cols", 0, 0, axis_index_groups=groups, tiled=True)

    both = jnp.stack([kv_first, kv_last])
    near = [both]
    for s in range(1, shifts):
        around = lambda r: (r & half_rows) | ((r + 2 * s) & (half_rows - 1))
        near.append(sent(both, "rows", around))
    near[-1], query_other = lax.optimization_barrier((near[-1], query_other))
    near = jnp.stack(near)
    far = sent(near, "rows", lambda r: r ^ 1)

    kept, partial, single_near, w_factors_near = pl.pallas_call(
        attend_kernel,
        out_shape=(
            jax.ShapeDtypeStruct((width + 8, tile_rows), f32),
            jax.ShapeDtypeStruct((width + 16, tile_rows), bf16),
            jax.ShapeDtypeStruct(single.shape, bf16),
            jax.ShapeDtypeStruct(w_factors.shape, bf16),
        ),
        in_specs=[in_hbm, in_hbm, in_vmem, in_vmem, in_hbm, in_hbm, in_hbm],
        scratch_shapes=[
            pltpu.VMEM((half_cols, tile_rows, tile_cols), f32),
            pltpu.VMEM(query.shape, f32),
            pltpu.VMEM(query.shape, f32),
            pltpu.VMEM(near.shape, bf16),
            pltpu.SemaphoreType.DMA((5,)),
        ],
        compiler_params=params(),
        name="attend",
    )(
        pinned(query),
        pinned(query_other),
        bias_heads,
        near,
        pinned(far),
        pinned(single),
        pinned(w_factors),
    )
    received = sent(partial, "cols", lambda c: c ^ half_cols)
    mixed = pl.pallas_call(
        join_kernel,
        out_shape=jax.ShapeDtypeStruct((cols, width, tile_rows), bf16),
        compiler_params=params(),
        name="join",
    )(kept, received)
    mixed_all = lax.all_to_all(mixed, "cols", 0, 0, tiled=True).reshape(single_width, tile_rows)

    single_out, factors, pairout_near, up_near, down_near = pl.pallas_call(
        factor_kernel,
        out_shape=(
            jax.ShapeDtypeStruct(single.shape, bf16),
            jax.ShapeDtypeStruct((tile_rows, w_factors.shape[1]), bf16),
            jax.ShapeDtypeStruct(w_pairout.shape, bf16),
            jax.ShapeDtypeStruct(w_up.shape, bf16),
            jax.ShapeDtypeStruct(w_down.shape, bf16),
        ),
        in_specs=[in_vmem] * 4 + [in_hbm] * 3,
        scratch_shapes=[pltpu.SemaphoreType.DMA((3,))],
        compiler_params=params(),
        name="factor",
    )(mixed_all, w_out, single_near, w_factors_near, pinned(w_pairout), pinned(w_up), pinned(w_down))

    targets = [nearest_rows(row, rows) for row in range(rows)]
    right_factors = sent(factors, both_axes, lambda r, c: (targets[r][c], r))

    block_rows = 32
    pair_block = pl.BlockSpec((block_rows, tile_cols, pair_width), lambda i: (i, 0, 0))
    updated = pl.pallas_call(
        update_kernel,
        grid=(tile_rows // block_rows,),
        in_specs=[pair_block] + [whole(factors.shape)] * 2 + [in_vmem] * 3,
        out_specs=pair_block,
        out_shape=jax.ShapeDtypeStruct(pair.shape, bf16),
        scratch_shapes=[
            pltpu.VMEM((tile_rows, 1, pair_width), bf16),
            pltpu.VMEM((tile_rows, 1, pair_width), bf16),
            pltpu.VMEM((tile_cols, pair_width), bf16),
        ],
        compiler_params=params(20),
        name="update",
    )(pair, factors, right_factors, pairout_near, up_near, down_near)
    return (single_out, updated)


def solution(mesh):
    return jax.shard_map(
        per_device,
        mesh=mesh,
        in_specs=(
            P("rows", None),
            P("rows", "cols", None),
            P(),
            P(),
            P(None, None, "cols"),
            P(),
            P(),
            P(),
            P(),
            P(),
        ),
        out_specs=(P("rows", None), P("rows", "cols", None)),
        check_vma=False,
    )
```

```python
import functools
import math

import jax
import jax.numpy as jnp
from jax import lax
from jax.experimental import pallas as pl
from jax.experimental.pallas import tpu as pltpu
from jax.sharding import PartitionSpec as P

epsilon = 1e-05
f32 = jnp.float32
bf16 = jnp.bfloat16
lowest = -1e30


def normalize(values):
    centred = values - jnp.mean(values, -1, keepdims=True)
    return centred * lax.rsqrt(jnp.mean(centred * centred, -1, keepdims=True) + epsilon)


def nt_dot(a, b):
    return lax.dot_general(a, b, (((1,), (1,)), ((), ())), preferred_element_type=f32)


def start_copies(pairs, sems):
    copies = [pltpu.make_async_copy(a, b, sems.at[i]) for i, (a, b) in enumerate(pairs)]
    for copy in copies:
        copy.start()
    return copies


def project_kernel(
    single_hbm, weight_hbm, query_ref, kv_ref, single_ref, weight_ref, sems
):
    copies = start_copies(((single_hbm, single_ref), (weight_hbm, weight_ref)), sems)
    copies[0].wait()
    normed = normalize(single_ref[...].astype(f32)).astype(bf16)
    copies[1].wait()
    projected = nt_dot(weight_ref[...], normed)
    width = query_ref.shape[0] // 2
    query_ref[:width] = projected[:width].astype(bf16)
    query_ref[width:] = jax.nn.sigmoid(projected[3 * width :]).astype(bf16)
    kv_ref[...] = projected[width : 3 * width].astype(bf16)


def normalize_rows(rounded):
    values = rounded.astype(f32)
    width = values.shape[-1]
    centred = values - jnp.dot(
        rounded, jnp.full((width, width), 1.0 / width, bf16), preferred_element_type=f32
    )
    square = jnp.mean(centred * centred, -1, keepdims=True)
    return (centred * lax.rsqrt(square + epsilon)).astype(bf16)


def bias_kernel(
    pair_hbm,
    weight_hbm,
    mask_hbm,
    out_hbm,
    pair_ref,
    weight_ref,
    mask_ref,
    held_ref,
    staged_ref,
    sems,
    out_sems,
):
    tile_rows, tile_cols, width = pair_ref.shape
    targets, heads_there = staged_ref.shape[:2]
    pairs = heads_there // 2
    ends = [tile_rows // 4, tile_rows]
    parts = [(weight_hbm, weight_ref), (mask_hbm.at[lax.axis_index("cols")], mask_ref)]
    at = 0
    for end in ends:
        rows_here = pl.ds(at, end - at)
        parts.append((pair_hbm.at[rows_here], pair_ref.at[rows_here]))
        at = end
    copies = start_copies(parts, sems)
    copies[0].wait()
    copies[1].wait()
    included = mask_ref[...] > 0
    at = 0
    outs = []
    for chunk, end in enumerate(ends):
        copies[2 + chunk].wait()
        step = end - at
        normed = normalize_rows(pair_ref[at:end].reshape(step * tile_cols, width))
        both = nt_dot(weight_ref[...], normed)
        for i in range(step):
            held_ref[:, i, :] = both[:, i * tile_cols : (i + 1) * tile_cols]
        held = jnp.where(included[None], held_ref[:, :step, :], lowest).astype(bf16)
        for d in range(targets):
            for p in range(heads_there // pairs):
                first = p * targets * pairs + d * pairs
                staged_ref[d, p * pairs : (p + 1) * pairs, at:end] = held[first : first + pairs]
        rows_here = pl.ds(at, step)
        out = pltpu.make_async_copy(
            staged_ref.at[:, :, rows_here], out_hbm.at[:, :, rows_here], out_sems.at[chunk]
        )
        out.start()
        outs.append(out)
        at = end
    for out in outs:
        out.wait()


def attend_kernel(
    own_ref,
    other_ref,
    bias_ref,
    near_ref,
    far_hbm,
    single_hbm,
    w_factors_hbm,
    w_pairout_hbm,
    w_up_hbm,
    w_down_hbm,
    kept_ref,
    sent_ref,
    single_ref,
    w_factors_ref,
    w_pairout_ref,
    w_up_ref,
    w_down_ref,
    score_ref,
    far_ref,
    sems,
):
    copies = start_copies(
        (
            (far_hbm, far_ref),
            (single_hbm, single_ref),
            (w_factors_hbm, w_factors_ref),
            (w_pairout_hbm, w_pairout_ref),
            (w_up_hbm, w_up_ref),
            (w_down_hbm, w_down_ref),
        ),
        sems,
    )
    blocks, heads_there, tile_rows, tile_cols = bias_ref.shape
    width = own_ref.shape[0] // 2
    pairs = heads_there // 2
    head_width = width // pairs
    score_scale = 1.0 / math.sqrt(head_width)
    shifts = near_ref.shape[0]
    row, col = lax.axis_index("rows"), lax.axis_index("cols")
    half, turn, core = row // (2 * shifts), (row // 2) % shifts, row % 2
    second = col // blocks

    def block(b, z, part):
        sent = (turn + shifts - b // 2) % shifts
        near, far = near_ref[sent, half ^ z, part, :], far_ref[sent, half ^ z, part, :]
        return jnp.where(core == b % 2, near, far)

    copies[0].wait()
    lane = lax.broadcasted_iota(jnp.int32, (tile_rows, 128), 1)
    for slot, query_ref in enumerate((own_ref, other_ref)):
        z = second ^ slot
        query = jnp.transpose(query_ref[:width].astype(f32)).astype(bf16)
        attended, sums = [], []
        for h in range(pairs):
            query_head = query[:, h * head_width : (h + 1) * head_width]
            key_rows = pl.ds(h * head_width, head_width)
            value_rows = pl.ds(width + h * head_width, head_width)
            top = None
            for b in range(blocks):
                scores = jnp.dot(query_head, block(b, z, key_rows), preferred_element_type=f32)
                scores = scores * score_scale + bias_ref[b, z * pairs + h].astype(f32)
                score_ref[b] = scores
                top = scores if top is None else jnp.maximum(top, scores)
            top = jnp.max(top, axis=-1, keepdims=True)
            total = mixed = None
            for b in range(blocks):
                weights = jnp.exp(score_ref[b] - top)
                part = nt_dot(weights.astype(bf16), block(b, z, value_rows))
                total = weights if total is None else total + weights
                mixed = part if mixed is None else mixed + part
            total = jnp.sum(total, axis=-1, keepdims=True)
            attended.append(mixed / total)
            sums.append(top + jnp.log(total))
        gated = jnp.transpose(jnp.concatenate(attended, axis=1)) * query_ref[width:].astype(f32)
        coded = jnp.zeros((tile_rows, 128), f32)
        for h, value in enumerate(sums):
            if slot == 0:
                coded = jnp.where(lane == h, value, coded)
                continue
            for p in range(3):
                part = value.astype(bf16).astype(f32)
                value = value - part
                coded = jnp.where(lane == p * pairs + h, part, coded)
        out_ref = sent_ref if slot else kept_ref
        out_ref[:width] = gated.astype(out_ref.dtype)
        out_ref[width:] = jnp.transpose(coded)[: out_ref.shape[0] - width].astype(out_ref.dtype)
    for copy in copies[1:]:
        copy.wait()


def join_kernel(kept_ref, received_ref, out_ref):
    width = out_ref.shape[1]
    pairs = 2
    head_width = width // pairs
    first = kept_ref[width : width + pairs]
    coded = received_ref[width:].astype(f32)
    last = coded[:pairs] + coded[pairs : 2 * pairs] + coded[2 * pairs : 3 * pairs]
    top = jnp.maximum(first, last)
    first, last = jnp.exp(first - top), jnp.exp(last - top)
    inverse = 1.0 / (first + last)
    first, last = first * inverse, last * inverse
    for h in range(pairs):
        here = pl.ds(h * head_width, head_width)
        joined = kept_ref[here] * first[h : h + 1]
        joined += received_ref[here].astype(f32) * last[h : h + 1]
        for d in range(out_ref.shape[0]):
            out_ref[d, here] = joined.astype(bf16)


def factor_kernel(mixed_ref, w_out_ref, single_ref, w_factors_ref, out_ref, factors_ref):
    mixed = jnp.transpose(mixed_ref[...].astype(f32)).astype(bf16)
    head_total = jnp.dot(mixed, w_out_ref[...], preferred_element_type=f32)
    single_out = (single_ref[...].astype(f32) + head_total).astype(bf16)
    out_ref[...] = single_out
    normed = normalize(single_out.astype(f32)).astype(bf16)
    factors_ref[...] = jnp.dot(normed, w_factors_ref[...], preferred_element_type=f32).astype(bf16)


def update_kernel(
    pair_ref,
    left_ref,
    right_factors_ref,
    w_pairout_ref,
    w_up_ref,
    w_down_ref,
    out_ref,
    scale_ref,
    shift_ref,
    right_ref,
):
    block_rows, tile_cols, width = pair_ref.shape
    factor_width = width // 2
    at = pl.program_id(0)

    @pl.when(at == 0)
    def _():
        right = right_factors_ref[:, factor_width:]
        right_ref[...] = jnp.concatenate([right, right], axis=1)
        left = left_ref[:, :factor_width].astype(f32)
        left = jnp.concatenate([left, left], axis=1)
        low = lax.broadcasted_iota(jnp.int32, (1, width), 1) < factor_width
        scale_ref[...] = jnp.where(low, left, -1.0).astype(bf16)[:, None, :]
        shift_ref[...] = jnp.where(low, 0.0, left).astype(bf16)[:, None, :]

    rows_here = block_rows * tile_cols
    here = pl.ds(at * block_rows, block_rows)
    paired = (right_ref[...][None] * scale_ref[here] + shift_ref[here]).reshape(rows_here, width)
    moved = jnp.dot(paired, w_pairout_ref[...], preferred_element_type=f32)
    pair_mid = (pair_ref[...].reshape(rows_here, width).astype(f32) + moved).astype(bf16)
    normed = normalize_rows(pair_mid)
    hidden = jnp.dot(normed, w_up_ref[...], preferred_element_type=f32).astype(bf16)
    hidden = jnp.maximum(hidden, 0)
    down = jnp.dot(hidden, w_down_ref[...], preferred_element_type=f32)
    out_ref[...] = (pair_mid.astype(f32) + down).astype(bf16).reshape(pair_ref.shape)


def nearest_rows(row, count):
    def ring(a, b, length):
        apart = abs(a - b) % length
        return min(apart, length - apart)

    def cost(col, target):
        z = (row // 8) * 4 + col // 4, (target // 8) * 4 + row // 4
        y = (row // 2) % 4, (target // 2) % 4
        apart = ring(*z, 8) + ring(*y, 4) + ring(col % 4, row % 4, 4) + 0.3 * (row % 2 != target % 2)
        return apart**4

    chosen = list(range(count))
    better = True
    while better:
        better = False
        for a in range(count):
            for b in range(a):
                now = cost(a, chosen[a]) + cost(b, chosen[b])
                if cost(a, chosen[b]) + cost(b, chosen[a]) < now - 1e-9:
                    chosen[a], chosen[b] = chosen[b], chosen[a]
                    better = True
    return chosen


def whole(shape):
    return pl.BlockSpec(shape, lambda *_: (0,) * len(shape))


def pinned(value):
    return pltpu.with_memory_space_constraint(value, pltpu.HBM)


def params(mib=8):
    return pltpu.CompilerParams(vmem_limit_bytes=mib * 1024 * 1024)


def per_device(
    single, pair, residue_mask, w_bias, w_project, w_out, w_factors, w_pairout, w_up, w_down
):
    tile_rows, tile_cols, pair_width = pair.shape
    single_width = single.shape[1]
    width = w_project.shape[2]
    rows, cols = lax.axis_size("rows"), lax.axis_size("cols")
    heads = w_bias.shape[1]
    in_place = pl.BlockSpec(memory_space=pl.ANY)
    in_hbm = pl.BlockSpec(memory_space=pltpu.HBM)
    in_vmem = pl.BlockSpec(memory_space=pltpu.VMEM)

    shifts = rows // 4
    half_rows, half_cols = rows // 2, cols // 2
    both_axes = ("rows", "cols")

    def sent(value, axes, target):
        if axes == "rows":
            routes = [(r, target(r)) for r in range(rows)]
        elif axes == "cols":
            routes = [(c, target(c)) for c in range(cols)]
        else:
            routes = []
            for r in range(rows):
                for c in range(cols):
                    to_row, to_col = target(r, c)
                    routes.append((r * cols + c, to_row * cols + to_col))
        return lax.ppermute(value, axes, routes)

    def rerouted(flip):
        def target(r, c):
            z_row, z_col = r // half_rows, c // half_cols
            return (z_col ^ flip) * half_rows + r % half_rows, z_row * half_cols + c % half_cols

        return target

    weight = jnp.transpose(w_project, (0, 2, 1)).reshape(4 * width, single_width)
    query, kv = pl.pallas_call(
        project_kernel,
        out_shape=(
            jax.ShapeDtypeStruct((2 * width, tile_rows), bf16),
            jax.ShapeDtypeStruct((2 * width, tile_rows), bf16),
        ),
        in_specs=[in_hbm, in_hbm],
        scratch_shapes=[
            pltpu.VMEM(single.shape, bf16),
            pltpu.VMEM(weight.shape, bf16),
            pltpu.SemaphoreType.DMA((2,)),
        ],
        compiler_params=params(),
        name="project",
    )(pinned(single), pinned(weight))

    kv_first = sent(kv, both_axes, rerouted(0))
    kv_last = sent(kv, both_axes, rerouted(1))
    kv, w_bias = lax.optimization_barrier((kv, w_bias))

    heads_there = 2 * heads // cols
    sent_shape = (half_cols, heads_there, tile_rows, tile_cols)
    bias_local = pl.pallas_call(
        bias_kernel,
        out_shape=jax.ShapeDtypeStruct(sent_shape, bf16),
        in_specs=[in_hbm, in_hbm, in_hbm],
        out_specs=in_place,
        scratch_shapes=[
            pltpu.VMEM(pair.shape, bf16),
            pltpu.VMEM((heads, pair_width), bf16),
            pltpu.VMEM((1, tile_cols), jnp.int32),
            pltpu.VMEM((heads, 3 * tile_rows // 4, tile_cols), f32),
            pltpu.VMEM(sent_shape, bf16),
            pltpu.SemaphoreType.DMA((4,)),
            pltpu.SemaphoreType.DMA((2,)),
        ],
        compiler_params=params(28),
        name="bias",
    )(pinned(pair), pinned(jnp.transpose(w_bias)), pinned(residue_mask.reshape(cols, 1, tile_cols)))
    query_other = sent(query, "cols", lambda c: c ^ half_cols)
    bias_local, kv_first, kv_last, query_other = lax.optimization_barrier(
        (bias_local, kv_first, kv_last, query_other)
    )
    groups = [list(range(half_cols)), list(range(half_cols, cols))]
    bias_heads = lax.all_to_all(bias_local, "cols", 0, 0, axis_index_groups=groups, tiled=True)

    both = jnp.stack([kv_first, kv_last])
    near = [both]
    for s in range(1, shifts):
        around = lambda r: (r & half_rows) | ((r + 2 * s) & (half_rows - 1))
        near.append(sent(both, "rows", around))
    near = jnp.stack(near)
    far = sent(near, "rows", lambda r: r ^ 1)

    kept, partial, single_near, factors_near, pairout_near, up_near, down_near = pl.pallas_call(
        attend_kernel,
        out_shape=(
            jax.ShapeDtypeStruct((width + 8, tile_rows), f32),
            jax.ShapeDtypeStruct((width + 16, tile_rows), bf16),
            jax.ShapeDtypeStruct(single.shape, bf16),
            jax.ShapeDtypeStruct(w_factors.shape, bf16),
            jax.ShapeDtypeStruct(w_pairout.shape, bf16),
            jax.ShapeDtypeStruct(w_up.shape, bf16),
            jax.ShapeDtypeStruct(w_down.shape, bf16),
        ),
        in_specs=[in_vmem] * 4 + [in_hbm] * 6,
        scratch_shapes=[
            pltpu.VMEM((half_cols, tile_rows, tile_cols), f32),
            pltpu.VMEM(near.shape, bf16),
            pltpu.SemaphoreType.DMA((6,)),
        ],
        compiler_params=params(),
        name="attend",
    )(
        query,
        query_other,
        bias_heads,
        near,
        pinned(far),
        pinned(single),
        pinned(w_factors),
        pinned(w_pairout),
        pinned(w_up),
        pinned(w_down),
    )
    received = sent(partial, "cols", lambda c: c ^ half_cols)
    mixed = pl.pallas_call(
        join_kernel,
        out_shape=jax.ShapeDtypeStruct((cols, width, tile_rows), bf16),
        compiler_params=params(),
        name="join",
    )(kept, received)
    mixed_all = lax.all_to_all(mixed, "cols", 0, 0, tiled=True).reshape(single_width, tile_rows)

    single_out, factors = pl.pallas_call(
        factor_kernel,
        out_shape=(
            jax.ShapeDtypeStruct(single.shape, bf16),
            jax.ShapeDtypeStruct((tile_rows, w_factors.shape[1]), bf16),
        ),
        compiler_params=params(),
        name="factor",
    )(mixed_all, w_out, single_near, factors_near)

    targets = [nearest_rows(row, rows) for row in range(rows)]
    right_factors = sent(factors, both_axes, lambda r, c: (targets[r][c], r))

    block_rows = 32
    pair_block = pl.BlockSpec((block_rows, tile_cols, pair_width), lambda i: (i, 0, 0))
    updated = pl.pallas_call(
        update_kernel,
        grid=(tile_rows // block_rows,),
        in_specs=[pair_block] + [whole(factors.shape)] * 2 + [in_vmem] * 3,
        out_specs=pair_block,
        out_shape=jax.ShapeDtypeStruct(pair.shape, bf16),
        scratch_shapes=[
            pltpu.VMEM((tile_rows, 1, pair_width), bf16),
            pltpu.VMEM((tile_rows, 1, pair_width), bf16),
            pltpu.VMEM((tile_cols, pair_width), bf16),
        ],
        compiler_params=params(20),
        name="update",
    )(pair, factors, right_factors, pairout_near, up_near, down_near)
    return (single_out, updated)


def solution(mesh):
    return jax.shard_map(
        per_device,
        mesh=mesh,
        in_specs=(
            P("rows", None),
            P("rows", "cols", None),
            P(),
            P(),
            P(None, None, "cols"),
            P(),
            P(),
            P(),
            P(),
            P(),
        ),
        out_specs=(P("rows", None), P("rows", "cols", None)),
        check_vma=False,
    )
```

```python
import functools
import math

import jax
import jax.numpy as jnp
from jax import lax
from jax.experimental import pallas as pl
from jax.experimental.pallas import tpu as pltpu
from jax.sharding import PartitionSpec as P

epsilon = 1e-05
f32 = jnp.float32
bf16 = jnp.bfloat16
lowest = -1e30


def normalize(values):
    centred = values - jnp.mean(values, -1, keepdims=True)
    return centred * lax.rsqrt(jnp.mean(centred * centred, -1, keepdims=True) + epsilon)


def nt_dot(a, b):
    return lax.dot_general(a, b, (((1,), (1,)), ((), ())), preferred_element_type=f32)


def start_copies(pairs, sems):
    copies = [pltpu.make_async_copy(a, b, sems.at[i]) for i, (a, b) in enumerate(pairs)]
    for copy in copies:
        copy.start()
    return copies


def project_kernel(
    single_hbm, weight_hbm, query_ref, kv_ref, single_ref, weight_ref, sems
):
    copies = start_copies(((single_hbm, single_ref), (weight_hbm, weight_ref)), sems)
    copies[0].wait()
    normed = normalize(single_ref[...].astype(f32)).astype(bf16)
    copies[1].wait()
    projected = nt_dot(weight_ref[...], normed)
    width = query_ref.shape[0] // 2
    query_ref[:width] = projected[:width].astype(bf16)
    query_ref[width:] = jax.nn.sigmoid(projected[3 * width :]).astype(bf16)
    kv_ref[...] = projected[width : 3 * width].astype(bf16)


def normalize_rows(rounded):
    values = rounded.astype(f32)
    width = values.shape[-1]
    centred = values - jnp.dot(
        rounded, jnp.full((width, width), 1.0 / width, bf16), preferred_element_type=f32
    )
    square = jnp.mean(centred * centred, -1, keepdims=True)
    return (centred * lax.rsqrt(square + epsilon)).astype(bf16)


def normalize_mixed(rounded, groups=8, across=4):
    size = rounded.shape[0] // groups
    parts = []
    for g in range(groups):
        rows_here = rounded[g * size : (g + 1) * size]
        if g % across == across - 1:
            parts.append(normalize(rows_here.astype(f32)).astype(bf16))
        else:
            parts.append(normalize_rows(rows_here))
    return jnp.concatenate(parts, axis=0)


def bias_kernel(
    pair_hbm,
    weight_hbm,
    mask_hbm,
    out_hbm,
    pair_ref,
    weight_ref,
    mask_ref,
    held_ref,
    staged_ref,
    sems,
    out_sems,
):
    tile_rows, tile_cols, width = pair_ref.shape
    targets, heads_there = staged_ref.shape[:2]
    pairs = heads_there // 2
    ends = [tile_rows // 4, tile_rows]
    parts = [(weight_hbm, weight_ref), (mask_hbm.at[lax.axis_index("cols")], mask_ref)]
    at = 0
    for end in ends:
        rows_here = pl.ds(at, end - at)
        parts.append((pair_hbm.at[rows_here], pair_ref.at[rows_here]))
        at = end
    copies = start_copies(parts, sems)
    copies[0].wait()
    copies[1].wait()
    included = mask_ref[...] > 0
    at = 0
    outs = []
    for chunk, end in enumerate(ends):
        copies[2 + chunk].wait()
        step = end - at
        normed = normalize_rows(pair_ref[at:end].reshape(step * tile_cols, width))
        both = nt_dot(weight_ref[...], normed)
        for i in range(step):
            held_ref[:, i, :] = both[:, i * tile_cols : (i + 1) * tile_cols]
        held = jnp.where(included[None], held_ref[:, :step, :], lowest).astype(bf16)
        for d in range(targets):
            for p in range(heads_there // pairs):
                first = p * targets * pairs + d * pairs
                staged_ref[d, p * pairs : (p + 1) * pairs, at:end] = held[first : first + pairs]
        rows_here = pl.ds(at, step)
        out = pltpu.make_async_copy(
            staged_ref.at[:, :, rows_here], out_hbm.at[:, :, rows_here], out_sems.at[chunk]
        )
        out.start()
        outs.append(out)
        at = end
    for out in outs:
        out.wait()


def attend_kernel(
    own_ref,
    other_ref,
    bias_ref,
    near_ref,
    far_hbm,
    single_hbm,
    w_factors_hbm,
    w_pairout_hbm,
    w_up_hbm,
    w_down_hbm,
    kept_ref,
    sent_ref,
    single_ref,
    w_factors_ref,
    w_pairout_ref,
    w_up_ref,
    w_down_ref,
    score_ref,
    far_ref,
    sems,
):
    copies = start_copies(
        (
            (far_hbm, far_ref),
            (single_hbm, single_ref),
            (w_factors_hbm, w_factors_ref),
            (w_pairout_hbm, w_pairout_ref),
            (w_up_hbm, w_up_ref),
            (w_down_hbm, w_down_ref),
        ),
        sems,
    )
    blocks, heads_there, tile_rows, tile_cols = bias_ref.shape
    width = own_ref.shape[0] // 2
    pairs = heads_there // 2
    head_width = width // pairs
    score_scale = 1.0 / math.sqrt(head_width)
    shifts = near_ref.shape[0]
    row, col = lax.axis_index("rows"), lax.axis_index("cols")
    half, turn, core = row // (2 * shifts), (row // 2) % shifts, row % 2
    second = col // blocks

    def block(b, z, part):
        sent = (turn + shifts - b // 2) % shifts
        near, far = near_ref[sent, half ^ z, part, :], far_ref[sent, half ^ z, part, :]
        return jnp.where(core == b % 2, near, far)

    queries = jnp.concatenate([own_ref[:width], other_ref[:width]], axis=0)
    queries = jnp.transpose(queries.astype(f32)).astype(bf16)
    copies[0].wait()
    lane = lax.broadcasted_iota(jnp.int32, (tile_rows, 128 - width), 1)
    for slot, query_ref in enumerate((own_ref, other_ref)):
        z = second ^ slot
        query = queries[:, slot * width : (slot + 1) * width]
        attended, sums = [], []
        for h in range(pairs):
            query_head = query[:, h * head_width : (h + 1) * head_width]
            key_rows = pl.ds(h * head_width, head_width)
            value_rows = pl.ds(width + h * head_width, head_width)
            top = None
            for b in range(blocks):
                scores = jnp.dot(query_head, block(b, z, key_rows), preferred_element_type=f32)
                scores = scores * score_scale + bias_ref[b, z * pairs + h].astype(f32)
                score_ref[b] = scores
                top = scores if top is None else jnp.maximum(top, scores)
            top = jnp.max(top, axis=-1, keepdims=True)
            total = mixed = None
            for b in range(blocks):
                weights = jnp.exp(score_ref[b] - top)
                part = nt_dot(weights.astype(bf16), block(b, z, value_rows))
                total = weights if total is None else total + weights
                mixed = part if mixed is None else mixed + part
            total = jnp.sum(total, axis=-1, keepdims=True)
            attended.append(mixed / total)
            sums.append(top + jnp.log(total))
        coded = jnp.zeros((tile_rows, 128 - width), f32)
        for h, value in enumerate(sums):
            if slot == 0:
                coded = jnp.where(lane == h, value, coded)
                continue
            for p in range(3):
                part = value.astype(bf16).astype(f32)
                value = value - part
                coded = jnp.where(lane == p * pairs + h, part, coded)
        turned = jnp.transpose(jnp.concatenate(attended + [coded], axis=1))
        out_ref = sent_ref if slot else kept_ref
        out_ref[:width] = (turned[:width] * query_ref[width:].astype(f32)).astype(out_ref.dtype)
        out_ref[width:] = turned[width : out_ref.shape[0]].astype(out_ref.dtype)
    for copy in copies[1:]:
        copy.wait()


def join_kernel(kept_ref, received_ref, out_ref):
    width = out_ref.shape[1]
    pairs = 2
    head_width = width // pairs
    first = kept_ref[width : width + pairs]
    coded = received_ref[width:].astype(f32)
    last = coded[:pairs] + coded[pairs : 2 * pairs] + coded[2 * pairs : 3 * pairs]
    top = jnp.maximum(first, last)
    first, last = jnp.exp(first - top), jnp.exp(last - top)
    inverse = 1.0 / (first + last)
    first, last = first * inverse, last * inverse
    for h in range(pairs):
        here = pl.ds(h * head_width, head_width)
        joined = kept_ref[here] * first[h : h + 1]
        joined += received_ref[here].astype(f32) * last[h : h + 1]
        for d in range(out_ref.shape[0]):
            out_ref[d, here] = joined.astype(bf16)


def factor_kernel(mixed_ref, w_out_ref, single_ref, w_factors_ref, out_ref, factors_ref):
    mixed = jnp.transpose(mixed_ref[...].astype(f32)).astype(bf16)
    head_total = jnp.dot(mixed, w_out_ref[...], preferred_element_type=f32)
    single_out = (single_ref[...].astype(f32) + head_total).astype(bf16)
    out_ref[...] = single_out
    normed = normalize(single_out.astype(f32)).astype(bf16)
    factors_ref[...] = jnp.dot(normed, w_factors_ref[...], preferred_element_type=f32).astype(bf16)


def update_kernel(
    pair_ref,
    left_ref,
    right_factors_ref,
    w_pairout_ref,
    w_up_ref,
    w_down_ref,
    out_ref,
    scale_ref,
    shift_ref,
    right_ref,
):
    block_rows, tile_cols, width = out_ref.shape
    factor_width = width // 2
    at = pl.program_id(0)

    @pl.when(at == 0)
    def _():
        right = right_factors_ref[:, factor_width:]
        right_ref[...] = jnp.concatenate([right, right], axis=1)
        left = left_ref[:, :factor_width].astype(f32)
        left = jnp.concatenate([left, left], axis=1)
        low = lax.broadcasted_iota(jnp.int32, (1, width), 1) < factor_width
        scale_ref[...] = jnp.where(low, left, -1.0).astype(bf16)[:, None, :]
        shift_ref[...] = jnp.where(low, 0.0, left).astype(bf16)[:, None, :]

    rows_here = block_rows * tile_cols
    here = pl.ds(at * block_rows, block_rows)
    paired = (right_ref[...][None] * scale_ref[here] + shift_ref[here]).reshape(rows_here, width)
    moved = jnp.dot(paired, w_pairout_ref[...], preferred_element_type=f32)
    pair_mid = (pair_ref[here].reshape(rows_here, width).astype(f32) + moved).astype(bf16)
    normed = normalize_mixed(pair_mid)
    hidden = jnp.dot(normed, w_up_ref[...], preferred_element_type=f32).astype(bf16)
    hidden = jnp.maximum(hidden, 0)
    down = jnp.dot(hidden, w_down_ref[...], preferred_element_type=f32)
    out_ref[...] = (pair_mid.astype(f32) + down).astype(bf16).reshape(out_ref.shape)


def nearest_rows(row, count):
    def ring(a, b, length):
        apart = abs(a - b) % length
        return min(apart, length - apart)

    def cost(col, target):
        z = (row // 8) * 4 + col // 4, (target // 8) * 4 + row // 4
        y = (row // 2) % 4, (target // 2) % 4
        apart = ring(*z, 8) + ring(*y, 4) + ring(col % 4, row % 4, 4) + 0.3 * (row % 2 != target % 2)
        return apart**4

    chosen = list(range(count))
    better = True
    while better:
        better = False
        for a in range(count):
            for b in range(a):
                now = cost(a, chosen[a]) + cost(b, chosen[b])
                if cost(a, chosen[b]) + cost(b, chosen[a]) < now - 1e-9:
                    chosen[a], chosen[b] = chosen[b], chosen[a]
                    better = True
    return chosen


def whole(shape):
    return pl.BlockSpec(shape, lambda *_: (0,) * len(shape))


def pinned(value):
    return pltpu.with_memory_space_constraint(value, pltpu.HBM)


def params(mib=8):
    return pltpu.CompilerParams(vmem_limit_bytes=mib * 1024 * 1024)


def per_device(
    single, pair, residue_mask, w_bias, w_project, w_out, w_factors, w_pairout, w_up, w_down
):
    tile_rows, tile_cols, pair_width = pair.shape
    single_width = single.shape[1]
    width = w_project.shape[2]
    rows, cols = lax.axis_size("rows"), lax.axis_size("cols")
    heads = w_bias.shape[1]
    in_place = pl.BlockSpec(memory_space=pl.ANY)
    in_hbm = pl.BlockSpec(memory_space=pltpu.HBM)
    in_vmem = pl.BlockSpec(memory_space=pltpu.VMEM)

    shifts = rows // 4
    half_rows, half_cols = rows // 2, cols // 2
    both_axes = ("rows", "cols")

    def sent(value, axes, target):
        if axes == "rows":
            routes = [(r, target(r)) for r in range(rows)]
        elif axes == "cols":
            routes = [(c, target(c)) for c in range(cols)]
        else:
            routes = []
            for r in range(rows):
                for c in range(cols):
                    to_row, to_col = target(r, c)
                    routes.append((r * cols + c, to_row * cols + to_col))
        return lax.ppermute(value, axes, routes)

    def rerouted(flip):
        def target(r, c):
            z_row, z_col = r // half_rows, c // half_cols
            return (z_col ^ flip) * half_rows + r % half_rows, z_row * half_cols + c % half_cols

        return target

    weight = jnp.transpose(w_project, (0, 2, 1)).reshape(4 * width, single_width)
    query, kv = pl.pallas_call(
        project_kernel,
        out_shape=(
            jax.ShapeDtypeStruct((2 * width, tile_rows), bf16),
            jax.ShapeDtypeStruct((2 * width, tile_rows), bf16),
        ),
        in_specs=[in_hbm, in_hbm],
        scratch_shapes=[
            pltpu.VMEM(single.shape, bf16),
            pltpu.VMEM(weight.shape, bf16),
            pltpu.SemaphoreType.DMA((2,)),
        ],
        compiler_params=params(),
        name="project",
    )(pinned(single), pinned(weight))

    kv_first = sent(kv, both_axes, rerouted(0))
    kv_last = sent(kv, both_axes, rerouted(1))
    kv, w_bias = lax.optimization_barrier((kv, w_bias))

    heads_there = 2 * heads // cols
    sent_shape = (half_cols, heads_there, tile_rows, tile_cols)
    bias_local = pl.pallas_call(
        bias_kernel,
        out_shape=jax.ShapeDtypeStruct(sent_shape, bf16),
        in_specs=[in_hbm, in_hbm, in_hbm],
        out_specs=in_place,
        scratch_shapes=[
            pltpu.VMEM(pair.shape, bf16),
            pltpu.VMEM((heads, pair_width), bf16),
            pltpu.VMEM((1, tile_cols), jnp.int32),
            pltpu.VMEM((heads, 3 * tile_rows // 4, tile_cols), f32),
            pltpu.VMEM(sent_shape, bf16),
            pltpu.SemaphoreType.DMA((4,)),
            pltpu.SemaphoreType.DMA((2,)),
        ],
        compiler_params=params(28),
        name="bias",
    )(pinned(pair), pinned(jnp.transpose(w_bias)), pinned(residue_mask.reshape(cols, 1, tile_cols)))
    query_other = sent(query, "cols", lambda c: c ^ half_cols)
    bias_local, kv_first, kv_last, query_other = lax.optimization_barrier(
        (bias_local, kv_first, kv_last, query_other)
    )
    groups = [list(range(half_cols)), list(range(half_cols, cols))]
    bias_heads = lax.all_to_all(bias_local, "cols", 0, 0, axis_index_groups=groups, tiled=True)

    both = jnp.stack([kv_first, kv_last])
    near = [both]
    for s in range(1, shifts):
        around = lambda r: (r & half_rows) | ((r + 2 * s) & (half_rows - 1))
        near.append(sent(both, "rows", around))
    near = jnp.stack(near)
    far = sent(near, "rows", lambda r: r ^ 1)

    kept, partial, single_near, factors_near, pairout_near, up_near, down_near = pl.pallas_call(
        attend_kernel,
        out_shape=(
            jax.ShapeDtypeStruct((width + 8, tile_rows), f32),
            jax.ShapeDtypeStruct((width + 16, tile_rows), bf16),
            jax.ShapeDtypeStruct(single.shape, bf16),
            jax.ShapeDtypeStruct(w_factors.shape, bf16),
            jax.ShapeDtypeStruct(w_pairout.shape, bf16),
            jax.ShapeDtypeStruct(w_up.shape, bf16),
            jax.ShapeDtypeStruct(w_down.shape, bf16),
        ),
        in_specs=[in_vmem] * 4 + [in_hbm] * 6,
        scratch_shapes=[
            pltpu.VMEM((half_cols, tile_rows, tile_cols), f32),
            pltpu.VMEM(near.shape, bf16),
            pltpu.SemaphoreType.DMA((6,)),
        ],
        compiler_params=params(),
        name="attend",
    )(
        query,
        query_other,
        bias_heads,
        near,
        pinned(far),
        pinned(single),
        pinned(w_factors),
        pinned(w_pairout),
        pinned(w_up),
        pinned(w_down),
    )
    received = sent(partial, "cols", lambda c: c ^ half_cols)
    mixed = pl.pallas_call(
        join_kernel,
        out_shape=jax.ShapeDtypeStruct((cols, width, tile_rows), bf16),
        compiler_params=params(),
        name="join",
    )(kept, received)
    mixed_all = lax.all_to_all(mixed, "cols", 0, 0, tiled=True).reshape(single_width, tile_rows)

    single_out, factors = pl.pallas_call(
        factor_kernel,
        out_shape=(
            jax.ShapeDtypeStruct(single.shape, bf16),
            jax.ShapeDtypeStruct((tile_rows, w_factors.shape[1]), bf16),
        ),
        compiler_params=params(),
        name="factor",
    )(mixed_all, w_out, single_near, factors_near)

    targets = [nearest_rows(row, rows) for row in range(rows)]
    right_factors = sent(factors, both_axes, lambda r, c: (targets[r][c], r))

    block_rows = 32
    pair_block = pl.BlockSpec((block_rows, tile_cols, pair_width), lambda i: (i, 0, 0))
    updated = pl.pallas_call(
        update_kernel,
        grid=(tile_rows // block_rows,),
        in_specs=[in_vmem] * 6,
        out_specs=pair_block,
        out_shape=jax.ShapeDtypeStruct(pair.shape, bf16),
        scratch_shapes=[
            pltpu.VMEM((tile_rows, 1, pair_width), bf16),
            pltpu.VMEM((tile_rows, 1, pair_width), bf16),
            pltpu.VMEM((tile_cols, pair_width), bf16),
        ],
        compiler_params=params(20),
        name="update",
    )(pair, factors, right_factors, pairout_near, up_near, down_near)
    return (single_out, updated)


def solution(mesh):
    return jax.shard_map(
        per_device,
        mesh=mesh,
        in_specs=(
            P("rows", None),
            P("rows", "cols", None),
            P(),
            P(),
            P(None, None, "cols"),
            P(),
            P(),
            P(),
            P(),
            P(),
        ),
        out_specs=(P("rows", None), P("rows", "cols", None)),
        check_vma=False,
    )
```

```python
import functools
import math

import jax
import jax.numpy as jnp
from jax import lax
from jax.experimental import pallas as pl
from jax.experimental.pallas import tpu as pltpu
from jax.sharding import PartitionSpec as P

epsilon = 1e-05
f32 = jnp.float32
bf16 = jnp.bfloat16
lowest = -1e30


def normalize(values):
    centred = values - jnp.mean(values, -1, keepdims=True)
    return centred * lax.rsqrt(jnp.mean(centred * centred, -1, keepdims=True) + epsilon)


def nt_dot(a, b):
    return lax.dot_general(a, b, (((1,), (1,)), ((), ())), preferred_element_type=f32)


def start_copies(pairs, sems):
    copies = [pltpu.make_async_copy(a, b, sems.at[i]) for i, (a, b) in enumerate(pairs)]
    for copy in copies:
        copy.start()
    return copies


def project_kernel(
    single_hbm, weight_hbm, pair_hbm, query_ref, kv_ref, pair_ref, single_ref, weight_ref, sems
):
    copies = start_copies(
        (
            (single_hbm, single_ref),
            (weight_hbm, weight_ref),
            (pair_hbm.at[pl.ds(0, pair_ref.shape[0])], pair_ref),
        ),
        sems,
    )
    copies[0].wait()
    normed = normalize(single_ref[...].astype(f32)).astype(bf16)
    copies[1].wait()
    projected = nt_dot(weight_ref[...], normed)
    width = query_ref.shape[0] // 2
    query_ref[:width] = projected[:width].astype(bf16)
    query_ref[width:] = jax.nn.sigmoid(projected[3 * width :]).astype(bf16)
    kv_ref[...] = projected[width : 3 * width].astype(bf16)
    copies[2].wait()


def normalize_rows(rounded):
    values = rounded.astype(f32)
    width = values.shape[-1]
    centred = values - jnp.dot(
        rounded, jnp.full((width, width), 1.0 / width, bf16), preferred_element_type=f32
    )
    square = jnp.mean(centred * centred, -1, keepdims=True)
    return (centred * lax.rsqrt(square + epsilon)).astype(bf16)


def normalize_mixed(rounded, groups=8, across=4):
    size = rounded.shape[0] // groups
    parts = []
    for g in range(groups):
        rows_here = rounded[g * size : (g + 1) * size]
        if g % across == across - 1:
            parts.append(normalize(rows_here.astype(f32)).astype(bf16))
        else:
            parts.append(normalize_rows(rows_here))
    return jnp.concatenate(parts, axis=0)


def bias_kernel(
    head_ref,
    pair_hbm,
    weight_hbm,
    mask_hbm,
    out_hbm,
    tail_ref,
    weight_ref,
    mask_ref,
    held_ref,
    staged_ref,
    sems,
    out_sems,
):
    head_rows, tile_cols, width = head_ref.shape
    tail_rows = tail_ref.shape[0]
    targets, heads_there = staged_ref.shape[:2]
    pairs = heads_there // 2
    copies = start_copies(
        (
            (weight_hbm, weight_ref),
            (mask_hbm.at[lax.axis_index("cols")], mask_ref),
            (pair_hbm.at[pl.ds(head_rows, tail_rows)], tail_ref),
        ),
        sems,
    )
    outs = []
    for chunk, (pair_ref, at) in enumerate(((head_ref, 0), (tail_ref, head_rows))):
        step = pair_ref.shape[0]
        if chunk:
            copies[2].wait()
        normed = normalize_rows(pair_ref[...].reshape(step * tile_cols, width))
        if not chunk:
            copies[0].wait()
            copies[1].wait()
            included = mask_ref[...] > 0
        both = nt_dot(weight_ref[...], normed)
        for i in range(step):
            held_ref[:, i, :] = both[:, i * tile_cols : (i + 1) * tile_cols]
        held = jnp.where(included[None], held_ref[:, :step, :], lowest).astype(bf16)
        for d in range(targets):
            for p in range(heads_there // pairs):
                first = p * targets * pairs + d * pairs
                staged_ref[d, p * pairs : (p + 1) * pairs, at : at + step] = held[
                    first : first + pairs
                ]
        rows_here = pl.ds(at, step)
        out = pltpu.make_async_copy(
            staged_ref.at[:, :, rows_here], out_hbm.at[:, :, rows_here], out_sems.at[chunk]
        )
        out.start()
        outs.append(out)
    for out in outs:
        out.wait()


def attend_kernel(
    own_ref,
    other_ref,
    bias_ref,
    near_ref,
    far_hbm,
    single_hbm,
    w_factors_hbm,
    w_pairout_hbm,
    w_up_hbm,
    w_down_hbm,
    kept_ref,
    sent_ref,
    single_ref,
    w_factors_ref,
    w_pairout_ref,
    w_up_ref,
    w_down_ref,
    score_ref,
    far_ref,
    sems,
):
    copies = start_copies(
        (
            (far_hbm, far_ref),
            (single_hbm, single_ref),
            (w_factors_hbm, w_factors_ref),
            (w_pairout_hbm, w_pairout_ref),
            (w_up_hbm, w_up_ref),
            (w_down_hbm, w_down_ref),
        ),
        sems,
    )
    blocks, heads_there, tile_rows, tile_cols = bias_ref.shape
    width = own_ref.shape[0] // 2
    pairs = heads_there // 2
    head_width = width // pairs
    score_scale = 1.0 / math.sqrt(head_width)
    shifts = near_ref.shape[0]
    row, col = lax.axis_index("rows"), lax.axis_index("cols")
    half, turn, core = row // (2 * shifts), (row // 2) % shifts, row % 2
    second = col // blocks

    def block(b, z, part):
        sent = (turn + shifts - b // 2) % shifts
        near, far = near_ref[sent, half ^ z, part, :], far_ref[sent, half ^ z, part, :]
        return jnp.where(core == b % 2, near, far)

    queries = jnp.concatenate([own_ref[:width], other_ref[:width]], axis=0)
    queries = jnp.transpose(queries.astype(f32)).astype(bf16)
    copies[0].wait()
    lane = lax.broadcasted_iota(jnp.int32, (tile_rows, 128 - width), 1)
    for slot, query_ref in enumerate((own_ref, other_ref)):
        z = second ^ slot
        query = queries[:, slot * width : (slot + 1) * width]
        attended, sums = [], []
        for h in range(pairs):
            query_head = query[:, h * head_width : (h + 1) * head_width]
            key_rows = pl.ds(h * head_width, head_width)
            value_rows = pl.ds(width + h * head_width, head_width)
            top = None
            for b in range(blocks):
                scores = jnp.dot(query_head, block(b, z, key_rows), preferred_element_type=f32)
                scores = scores * score_scale + bias_ref[b, z * pairs + h].astype(f32)
                score_ref[b] = scores
                top = scores if top is None else jnp.maximum(top, scores)
            top = jnp.max(top, axis=-1, keepdims=True)
            total = mixed = None
            for b in range(blocks):
                weights = jnp.exp(score_ref[b] - top)
                part = nt_dot(weights.astype(bf16), block(b, z, value_rows))
                total = weights if total is None else total + weights
                mixed = part if mixed is None else mixed + part
            total = jnp.sum(total, axis=-1, keepdims=True)
            attended.append(mixed / total)
            sums.append(top + jnp.log(total))
        coded = jnp.zeros((tile_rows, 128 - width), f32)
        for h, value in enumerate(sums):
            if slot == 0:
                coded = jnp.where(lane == h, value, coded)
                continue
            for p in range(3):
                part = value.astype(bf16).astype(f32)
                value = value - part
                coded = jnp.where(lane == p * pairs + h, part, coded)
        turned = jnp.transpose(jnp.concatenate(attended + [coded], axis=1))
        out_ref = sent_ref if slot else kept_ref
        out_ref[:width] = (turned[:width] * query_ref[width:].astype(f32)).astype(out_ref.dtype)
        out_ref[width:] = turned[width : out_ref.shape[0]].astype(out_ref.dtype)
    for copy in copies[1:]:
        copy.wait()


def join_kernel(kept_ref, received_ref, out_ref):
    width = out_ref.shape[1]
    pairs = 2
    head_width = width // pairs
    first = kept_ref[width : width + pairs]
    coded = received_ref[width:].astype(f32)
    last = coded[:pairs] + coded[pairs : 2 * pairs] + coded[2 * pairs : 3 * pairs]
    top = jnp.maximum(first, last)
    first, last = jnp.exp(first - top), jnp.exp(last - top)
    inverse = 1.0 / (first + last)
    first, last = first * inverse, last * inverse
    for h in range(pairs):
        here = pl.ds(h * head_width, head_width)
        joined = kept_ref[here] * first[h : h + 1]
        joined += received_ref[here].astype(f32) * last[h : h + 1]
        for d in range(out_ref.shape[0]):
            out_ref[d, here] = joined.astype(bf16)


def factor_kernel(mixed_ref, w_out_ref, single_ref, w_factors_ref, out_ref, factors_ref):
    mixed = jnp.transpose(mixed_ref[...].astype(f32)).astype(bf16)
    head_total = jnp.dot(mixed, w_out_ref[...], preferred_element_type=f32)
    single_out = (single_ref[...].astype(f32) + head_total).astype(bf16)
    out_ref[...] = single_out
    normed = normalize(single_out.astype(f32)).astype(bf16)
    factors_ref[...] = jnp.dot(normed, w_factors_ref[...], preferred_element_type=f32).astype(bf16)


def update_kernel(
    pair_ref,
    left_ref,
    right_factors_ref,
    w_pairout_ref,
    w_up_ref,
    w_down_ref,
    out_ref,
    scale_ref,
    shift_ref,
    right_ref,
):
    block_rows, tile_cols, width = out_ref.shape
    factor_width = width // 2
    at = pl.program_id(0)

    @pl.when(at == 0)
    def _():
        right = right_factors_ref[:, factor_width:]
        right_ref[...] = jnp.concatenate([right, right], axis=1)
        left = left_ref[:, :factor_width].astype(f32)
        left = jnp.concatenate([left, left], axis=1)
        low = lax.broadcasted_iota(jnp.int32, (1, width), 1) < factor_width
        scale_ref[...] = jnp.where(low, left, -1.0).astype(bf16)[:, None, :]
        shift_ref[...] = jnp.where(low, 0.0, left).astype(bf16)[:, None, :]

    rows_here = block_rows * tile_cols
    here = pl.ds(at * block_rows, block_rows)
    paired = (right_ref[...][None] * scale_ref[here] + shift_ref[here]).reshape(rows_here, width)
    moved = jnp.dot(paired, w_pairout_ref[...], preferred_element_type=f32)
    pair_mid = (pair_ref[here].reshape(rows_here, width).astype(f32) + moved).astype(bf16)
    normed = normalize_mixed(pair_mid)
    hidden = jnp.dot(normed, w_up_ref[...], preferred_element_type=f32).astype(bf16)
    hidden = jnp.maximum(hidden, 0)
    down = jnp.dot(hidden, w_down_ref[...], preferred_element_type=f32)
    out_ref[...] = (pair_mid.astype(f32) + down).astype(bf16).reshape(out_ref.shape)


def nearest_rows(row, count):
    def ring(a, b, length):
        apart = abs(a - b) % length
        return min(apart, length - apart)

    def cost(col, target):
        z = (row // 8) * 4 + col // 4, (target // 8) * 4 + row // 4
        y = (row // 2) % 4, (target // 2) % 4
        apart = ring(*z, 8) + ring(*y, 4) + ring(col % 4, row % 4, 4) + 0.3 * (row % 2 != target % 2)
        return apart**4

    chosen = list(range(count))
    better = True
    while better:
        better = False
        for a in range(count):
            for b in range(a):
                now = cost(a, chosen[a]) + cost(b, chosen[b])
                if cost(a, chosen[b]) + cost(b, chosen[a]) < now - 1e-9:
                    chosen[a], chosen[b] = chosen[b], chosen[a]
                    better = True
    return chosen


def whole(shape):
    return pl.BlockSpec(shape, lambda *_: (0,) * len(shape))


def pinned(value):
    return pltpu.with_memory_space_constraint(value, pltpu.HBM)


def params(mib=8):
    return pltpu.CompilerParams(vmem_limit_bytes=mib * 1024 * 1024)


def per_device(
    single, pair, residue_mask, w_bias, w_project, w_out, w_factors, w_pairout, w_up, w_down
):
    tile_rows, tile_cols, pair_width = pair.shape
    single_width = single.shape[1]
    width = w_project.shape[2]
    rows, cols = lax.axis_size("rows"), lax.axis_size("cols")
    heads = w_bias.shape[1]
    in_place = pl.BlockSpec(memory_space=pl.ANY)
    in_hbm = pl.BlockSpec(memory_space=pltpu.HBM)
    in_vmem = pl.BlockSpec(memory_space=pltpu.VMEM)

    shifts = rows // 4
    half_rows, half_cols = rows // 2, cols // 2
    both_axes = ("rows", "cols")

    def sent(value, axes, target):
        if axes == "rows":
            routes = [(r, target(r)) for r in range(rows)]
        elif axes == "cols":
            routes = [(c, target(c)) for c in range(cols)]
        else:
            routes = []
            for r in range(rows):
                for c in range(cols):
                    to_row, to_col = target(r, c)
                    routes.append((r * cols + c, to_row * cols + to_col))
        return lax.ppermute(value, axes, routes)

    def rerouted(flip):
        def target(r, c):
            z_row, z_col = r // half_rows, c // half_cols
            return (z_col ^ flip) * half_rows + r % half_rows, z_row * half_cols + c % half_cols

        return target

    weight = jnp.transpose(w_project, (0, 2, 1)).reshape(4 * width, single_width)
    head_rows = tile_rows // 4
    query, kv, pair_head = pl.pallas_call(
        project_kernel,
        out_shape=(
            jax.ShapeDtypeStruct((2 * width, tile_rows), bf16),
            jax.ShapeDtypeStruct((2 * width, tile_rows), bf16),
            jax.ShapeDtypeStruct((head_rows, tile_cols, pair_width), bf16),
        ),
        in_specs=[in_hbm, in_hbm, in_hbm],
        scratch_shapes=[
            pltpu.VMEM(single.shape, bf16),
            pltpu.VMEM(weight.shape, bf16),
            pltpu.SemaphoreType.DMA((3,)),
        ],
        compiler_params=params(),
        name="project",
    )(pinned(single), pinned(weight), pinned(pair))

    kv_first = sent(kv, both_axes, rerouted(0))
    kv_last = sent(kv, both_axes, rerouted(1))
    kv, w_bias = lax.optimization_barrier((kv, w_bias))

    heads_there = 2 * heads // cols
    sent_shape = (half_cols, heads_there, tile_rows, tile_cols)
    bias_local = pl.pallas_call(
        bias_kernel,
        out_shape=jax.ShapeDtypeStruct(sent_shape, bf16),
        in_specs=[in_vmem, in_hbm, in_hbm, in_hbm],
        out_specs=in_place,
        scratch_shapes=[
            pltpu.VMEM((tile_rows - head_rows, tile_cols, pair_width), bf16),
            pltpu.VMEM((heads, pair_width), bf16),
            pltpu.VMEM((1, tile_cols), jnp.int32),
            pltpu.VMEM((heads, tile_rows - head_rows, tile_cols), f32),
            pltpu.VMEM(sent_shape, bf16),
            pltpu.SemaphoreType.DMA((3,)),
            pltpu.SemaphoreType.DMA((2,)),
        ],
        compiler_params=params(28),
        name="bias",
    )(
        pair_head,
        pinned(pair),
        pinned(jnp.transpose(w_bias)),
        pinned(residue_mask.reshape(cols, 1, tile_cols)),
    )
    query_other = sent(query, "cols", lambda c: c ^ half_cols)
    bias_local, kv_first, kv_last, query_other = lax.optimization_barrier(
        (bias_local, kv_first, kv_last, query_other)
    )
    groups = [list(range(half_cols)), list(range(half_cols, cols))]
    bias_heads = lax.all_to_all(bias_local, "cols", 0, 0, axis_index_groups=groups, tiled=True)

    both = jnp.stack([kv_first, kv_last])
    near = [both]
    for s in range(1, shifts):
        around = lambda r: (r & half_rows) | ((r + 2 * s) & (half_rows - 1))
        near.append(sent(both, "rows", around))
    near = jnp.stack(near)
    far = sent(near, "rows", lambda r: r ^ 1)

    kept, partial, single_near, factors_near, pairout_near, up_near, down_near = pl.pallas_call(
        attend_kernel,
        out_shape=(
            jax.ShapeDtypeStruct((width + 8, tile_rows), f32),
            jax.ShapeDtypeStruct((width + 16, tile_rows), bf16),
            jax.ShapeDtypeStruct(single.shape, bf16),
            jax.ShapeDtypeStruct(w_factors.shape, bf16),
            jax.ShapeDtypeStruct(w_pairout.shape, bf16),
            jax.ShapeDtypeStruct(w_up.shape, bf16),
            jax.ShapeDtypeStruct(w_down.shape, bf16),
        ),
        in_specs=[in_vmem] * 4 + [in_hbm] * 6,
        scratch_shapes=[
            pltpu.VMEM((half_cols, tile_rows, tile_cols), f32),
            pltpu.VMEM(near.shape, bf16),
            pltpu.SemaphoreType.DMA((6,)),
        ],
        compiler_params=params(),
        name="attend",
    )(
        query,
        query_other,
        bias_heads,
        near,
        pinned(far),
        pinned(single),
        pinned(w_factors),
        pinned(w_pairout),
        pinned(w_up),
        pinned(w_down),
    )
    received = sent(partial, "cols", lambda c: c ^ half_cols)
    mixed = pl.pallas_call(
        join_kernel,
        out_shape=jax.ShapeDtypeStruct((cols, width, tile_rows), bf16),
        compiler_params=params(),
        name="join",
    )(kept, received)
    mixed_all = lax.all_to_all(mixed, "cols", 0, 0, tiled=True).reshape(single_width, tile_rows)

    single_out, factors = pl.pallas_call(
        factor_kernel,
        out_shape=(
            jax.ShapeDtypeStruct(single.shape, bf16),
            jax.ShapeDtypeStruct((tile_rows, w_factors.shape[1]), bf16),
        ),
        compiler_params=params(),
        name="factor",
    )(mixed_all, w_out, single_near, factors_near)

    targets = [nearest_rows(row, rows) for row in range(rows)]
    right_factors = sent(factors, both_axes, lambda r, c: (targets[r][c], r))

    block_rows = 32
    pair_block = pl.BlockSpec((block_rows, tile_cols, pair_width), lambda i: (i, 0, 0))
    updated = pl.pallas_call(
        update_kernel,
        grid=(tile_rows // block_rows,),
        in_specs=[in_vmem] * 6,
        out_specs=pair_block,
        out_shape=jax.ShapeDtypeStruct(pair.shape, bf16),
        scratch_shapes=[
            pltpu.VMEM((tile_rows, 1, pair_width), bf16),
            pltpu.VMEM((tile_rows, 1, pair_width), bf16),
            pltpu.VMEM((tile_cols, pair_width), bf16),
        ],
        compiler_params=params(20),
        name="update",
    )(pair, factors, right_factors, pairout_near, up_near, down_near)
    return (single_out, updated)


def solution(mesh):
    return jax.shard_map(
        per_device,
        mesh=mesh,
        in_specs=(
            P("rows", None),
            P("rows", "cols", None),
            P(),
            P(),
            P(None, None, "cols"),
            P(),
            P(),
            P(),
            P(),
            P(),
        ),
        out_specs=(P("rows", None), P("rows", "cols", None)),
        check_vma=False,
    )
```

```python
import functools
import math

import jax
import jax.numpy as jnp
from jax import lax
from jax.experimental import pallas as pl
from jax.experimental.pallas import tpu as pltpu
from jax.sharding import PartitionSpec as P

epsilon = 1e-05
f32 = jnp.float32
bf16 = jnp.bfloat16
lowest = -1e30


def normalize(values):
    centred = values - jnp.mean(values, -1, keepdims=True)
    return centred * lax.rsqrt(jnp.mean(centred * centred, -1, keepdims=True) + epsilon)


def nt_dot(a, b):
    return lax.dot_general(a, b, (((1,), (1,)), ((), ())), preferred_element_type=f32)


def start_copies(pairs, sems):
    copies = [pltpu.make_async_copy(a, b, sems.at[i]) for i, (a, b) in enumerate(pairs)]
    for copy in copies:
        copy.start()
    return copies


def project_kernel(
    single_hbm, weight_hbm, query_ref, kv_ref, single_ref, weight_ref, sems
):
    copies = start_copies(((single_hbm, single_ref), (weight_hbm, weight_ref)), sems)
    copies[0].wait()
    normed = normalize(single_ref[...].astype(f32)).astype(bf16)
    copies[1].wait()
    projected = nt_dot(weight_ref[...], normed)
    width = query_ref.shape[0] // 2
    query_ref[:width] = projected[:width].astype(bf16)
    query_ref[width:] = jax.nn.sigmoid(projected[3 * width :]).astype(bf16)
    kv_ref[...] = projected[width : 3 * width].astype(bf16)


def normalize_rows(rounded):
    values = rounded.astype(f32)
    width = values.shape[-1]
    centred = values - jnp.dot(
        rounded, jnp.full((width, width), 1.0 / width, bf16), preferred_element_type=f32
    )
    square = jnp.mean(centred * centred, -1, keepdims=True)
    return (centred * lax.rsqrt(square + epsilon)).astype(bf16)


def normalize_mixed(rounded, groups=8, across=4):
    size = rounded.shape[0] // groups
    parts = []
    for g in range(groups):
        rows_here = rounded[g * size : (g + 1) * size]
        if g % across == across - 1:
            parts.append(normalize(rows_here.astype(f32)).astype(bf16))
        else:
            parts.append(normalize_rows(rows_here))
    return jnp.concatenate(parts, axis=0)


def bias_kernel(
    pair_hbm,
    weight_hbm,
    mask_hbm,
    out_hbm,
    pair_ref,
    weight_ref,
    mask_ref,
    held_ref,
    staged_ref,
    sems,
    out_sems,
):
    tile_rows, tile_cols, width = pair_ref.shape
    targets, heads_there = staged_ref.shape[:2]
    pairs = heads_there // 2
    ends = [tile_rows // 4, tile_rows]
    parts = [(weight_hbm, weight_ref), (mask_hbm.at[lax.axis_index("cols")], mask_ref)]
    at = 0
    for end in ends:
        rows_here = pl.ds(at, end - at)
        parts.append((pair_hbm.at[rows_here], pair_ref.at[rows_here]))
        at = end
    copies = start_copies(parts, sems)
    copies[0].wait()
    copies[1].wait()
    included = mask_ref[...] > 0
    at = 0
    outs = []
    for chunk, end in enumerate(ends):
        copies[2 + chunk].wait()
        step = end - at
        normed = normalize_rows(pair_ref[at:end].reshape(step * tile_cols, width))
        both = nt_dot(weight_ref[...], normed)
        for i in range(step):
            held_ref[:, i, :] = both[:, i * tile_cols : (i + 1) * tile_cols]
        held = jnp.where(included[None], held_ref[:, :step, :], lowest).astype(bf16)
        for d in range(targets):
            for p in range(heads_there // pairs):
                first = p * targets * pairs + d * pairs
                staged_ref[d, p * pairs : (p + 1) * pairs, at:end] = held[first : first + pairs]
        rows_here = pl.ds(at, step)
        out = pltpu.make_async_copy(
            staged_ref.at[:, :, rows_here], out_hbm.at[:, :, rows_here], out_sems.at[chunk]
        )
        out.start()
        outs.append(out)
        at = end
    for out in outs:
        out.wait()


def attend_kernel(
    own_ref,
    other_ref,
    bias_ref,
    kv_ref,
    single_hbm,
    w_factors_hbm,
    w_pairout_hbm,
    w_up_hbm,
    w_down_hbm,
    w_out_hbm,
    kept_ref,
    sent_ref,
    single_ref,
    w_factors_ref,
    w_pairout_ref,
    w_up_ref,
    w_down_ref,
    w_out_ref,
    score_ref,
    sems,
):
    copies = start_copies(
        (
            (single_hbm, single_ref),
            (w_factors_hbm, w_factors_ref),
            (w_out_hbm, w_out_ref),
            (w_pairout_hbm, w_pairout_ref),
            (w_up_hbm, w_up_ref),
            (w_down_hbm, w_down_ref),
        ),
        sems,
    )
    blocks, heads_there, tile_rows, tile_cols = bias_ref.shape
    width = own_ref.shape[0] // 2
    pairs = heads_there // 2
    head_width = width // pairs
    score_scale = 1.0 / math.sqrt(head_width)
    shifts = kv_ref.shape[1]
    row, col = lax.axis_index("rows"), lax.axis_index("cols")
    half, turn, core = row // (2 * shifts), (row // 2) % shifts, row % 2
    second = col // blocks

    def block(b, z, part):
        sent = (turn + shifts - b // 2) % shifts
        return kv_ref[(b % 2) ^ core, sent, half ^ z, part, :]

    queries = jnp.concatenate([own_ref[:width], other_ref[:width]], axis=0)
    queries = jnp.transpose(queries.astype(f32)).astype(bf16)
    lane = lax.broadcasted_iota(jnp.int32, (tile_rows, 128 - width), 1)
    for slot, query_ref in enumerate((own_ref, other_ref)):
        z = second ^ slot
        query = queries[:, slot * width : (slot + 1) * width]
        attended, sums = [], []
        for h in range(pairs):
            query_head = query[:, h * head_width : (h + 1) * head_width]
            key_rows = pl.ds(h * head_width, head_width)
            value_rows = pl.ds(width + h * head_width, head_width)
            top = None
            for b in range(blocks):
                scores = jnp.dot(query_head, block(b, z, key_rows), preferred_element_type=f32)
                scores = scores * score_scale + bias_ref[b, z * pairs + h].astype(f32)
                score_ref[b] = scores
                top = scores if top is None else jnp.maximum(top, scores)
            top = jnp.max(top, axis=-1, keepdims=True)
            total = mixed = None
            for b in range(blocks):
                weights = jnp.exp(score_ref[b] - top)
                part = nt_dot(weights.astype(bf16), block(b, z, value_rows))
                total = weights if total is None else total + weights
                mixed = part if mixed is None else mixed + part
            total = jnp.sum(total, axis=-1, keepdims=True)
            attended.append(mixed / total)
            sums.append(top + jnp.log(total))
        coded = jnp.zeros((tile_rows, 128 - width), f32)
        for h, value in enumerate(sums):
            if slot == 0:
                coded = jnp.where(lane == h, value, coded)
                continue
            for p in range(3):
                part = value.astype(bf16).astype(f32)
                value = value - part
                coded = jnp.where(lane == p * pairs + h, part, coded)
        turned = jnp.transpose(jnp.concatenate(attended + [coded], axis=1))
        out_ref = sent_ref if slot else kept_ref
        out_ref[:width] = (turned[:width] * query_ref[width:].astype(f32)).astype(out_ref.dtype)
        out_ref[width:] = turned[width : out_ref.shape[0]].astype(out_ref.dtype)
    for copy in copies:
        copy.wait()


def join_kernel(kept_ref, received_ref, out_ref):
    width = out_ref.shape[1]
    pairs = 2
    head_width = width // pairs
    first = kept_ref[width : width + pairs]
    coded = received_ref[width:].astype(f32)
    last = coded[:pairs] + coded[pairs : 2 * pairs] + coded[2 * pairs : 3 * pairs]
    top = jnp.maximum(first, last)
    first, last = jnp.exp(first - top), jnp.exp(last - top)
    inverse = 1.0 / (first + last)
    first, last = first * inverse, last * inverse
    for h in range(pairs):
        here = pl.ds(h * head_width, head_width)
        joined = kept_ref[here] * first[h : h + 1]
        joined += received_ref[here].astype(f32) * last[h : h + 1]
        for d in range(out_ref.shape[0]):
            out_ref[d, here] = joined.astype(bf16)


def factor_kernel(mixed_ref, w_out_ref, single_ref, w_factors_ref, out_ref, factors_ref):
    mixed = jnp.transpose(mixed_ref[...].astype(f32)).astype(bf16)
    head_total = jnp.dot(mixed, w_out_ref[...], preferred_element_type=f32)
    single_out = (single_ref[...].astype(f32) + head_total).astype(bf16)
    out_ref[...] = single_out
    normed = normalize(single_out.astype(f32)).astype(bf16)
    factors_ref[...] = jnp.dot(normed, w_factors_ref[...], preferred_element_type=f32).astype(bf16)


def update_kernel(
    pair_ref,
    left_ref,
    right_factors_ref,
    w_pairout_ref,
    w_up_ref,
    w_down_ref,
    out_ref,
    scale_ref,
    shift_ref,
    right_ref,
):
    block_rows, tile_cols, width = out_ref.shape
    factor_width = width // 2
    at = pl.program_id(0)

    @pl.when(at == 0)
    def _():
        right = right_factors_ref[:, factor_width:]
        right_ref[...] = jnp.concatenate([right, right], axis=1)
        left = left_ref[:, :factor_width].astype(f32)
        left = jnp.concatenate([left, left], axis=1)
        low = lax.broadcasted_iota(jnp.int32, (1, width), 1) < factor_width
        scale_ref[...] = jnp.where(low, left, -1.0).astype(bf16)[:, None, :]
        shift_ref[...] = jnp.where(low, 0.0, left).astype(bf16)[:, None, :]

    rows_here = block_rows * tile_cols
    here = pl.ds(at * block_rows, block_rows)
    paired = (right_ref[...][None] * scale_ref[here] + shift_ref[here]).reshape(rows_here, width)
    moved = jnp.dot(paired, w_pairout_ref[...], preferred_element_type=f32)
    pair_mid = (pair_ref[here].reshape(rows_here, width).astype(f32) + moved).astype(bf16)
    normed = normalize_mixed(pair_mid)
    hidden = jnp.dot(normed, w_up_ref[...], preferred_element_type=f32).astype(bf16)
    hidden = jnp.maximum(hidden, 0)
    down = jnp.dot(hidden, w_down_ref[...], preferred_element_type=f32)
    out_ref[...] = (pair_mid.astype(f32) + down).astype(bf16).reshape(out_ref.shape)


def nearest_rows(row, count):
    def ring(a, b, length):
        apart = abs(a - b) % length
        return min(apart, length - apart)

    def cost(col, target):
        z = (row // 8) * 4 + col // 4, (target // 8) * 4 + row // 4
        y = (row // 2) % 4, (target // 2) % 4
        apart = ring(*z, 8) + ring(*y, 4) + ring(col % 4, row % 4, 4) + 0.3 * (row % 2 != target % 2)
        return apart**4

    chosen = list(range(count))
    better = True
    while better:
        better = False
        for a in range(count):
            for b in range(a):
                now = cost(a, chosen[a]) + cost(b, chosen[b])
                if cost(a, chosen[b]) + cost(b, chosen[a]) < now - 1e-9:
                    chosen[a], chosen[b] = chosen[b], chosen[a]
                    better = True
    return chosen


def whole(shape):
    return pl.BlockSpec(shape, lambda *_: (0,) * len(shape))


def pinned(value):
    return pltpu.with_memory_space_constraint(value, pltpu.HBM)


def params(mib=8):
    return pltpu.CompilerParams(vmem_limit_bytes=mib * 1024 * 1024)


def per_device(
    single, pair, residue_mask, w_bias, w_project, w_out, w_factors, w_pairout, w_up, w_down
):
    tile_rows, tile_cols, pair_width = pair.shape
    single_width = single.shape[1]
    width = w_project.shape[2]
    rows, cols = lax.axis_size("rows"), lax.axis_size("cols")
    heads = w_bias.shape[1]
    in_place = pl.BlockSpec(memory_space=pl.ANY)
    in_hbm = pl.BlockSpec(memory_space=pltpu.HBM)
    in_vmem = pl.BlockSpec(memory_space=pltpu.VMEM)

    shifts = rows // 4
    half_rows, half_cols = rows // 2, cols // 2
    both_axes = ("rows", "cols")

    def sent(value, axes, target):
        if axes == "rows":
            routes = [(r, target(r)) for r in range(rows)]
        elif axes == "cols":
            routes = [(c, target(c)) for c in range(cols)]
        else:
            routes = []
            for r in range(rows):
                for c in range(cols):
                    to_row, to_col = target(r, c)
                    routes.append((r * cols + c, to_row * cols + to_col))
        return lax.ppermute(value, axes, routes)

    def rerouted(flip):
        def target(r, c):
            z_row, z_col = r // half_rows, c // half_cols
            return (z_col ^ flip) * half_rows + r % half_rows, z_row * half_cols + c % half_cols

        return target

    weight = jnp.transpose(w_project, (0, 2, 1)).reshape(4 * width, single_width)
    query, kv = pl.pallas_call(
        project_kernel,
        out_shape=(
            jax.ShapeDtypeStruct((2 * width, tile_rows), bf16),
            jax.ShapeDtypeStruct((2 * width, tile_rows), bf16),
        ),
        in_specs=[in_hbm, in_hbm],
        scratch_shapes=[
            pltpu.VMEM(single.shape, bf16),
            pltpu.VMEM(weight.shape, bf16),
            pltpu.SemaphoreType.DMA((2,)),
        ],
        compiler_params=params(),
        name="project",
    )(pinned(single), pinned(weight))

    kv_first = sent(kv, both_axes, rerouted(0))
    kv_last = sent(kv, both_axes, rerouted(1))
    kv, w_bias = lax.optimization_barrier((kv, w_bias))

    heads_there = 2 * heads // cols
    sent_shape = (half_cols, heads_there, tile_rows, tile_cols)
    bias_local = pl.pallas_call(
        bias_kernel,
        out_shape=jax.ShapeDtypeStruct(sent_shape, bf16),
        in_specs=[in_hbm, in_hbm, in_hbm],
        out_specs=in_place,
        scratch_shapes=[
            pltpu.VMEM(pair.shape, bf16),
            pltpu.VMEM((heads, pair_width), bf16),
            pltpu.VMEM((1, tile_cols), jnp.int32),
            pltpu.VMEM((heads, 3 * tile_rows // 4, tile_cols), f32),
            pltpu.VMEM(sent_shape, bf16),
            pltpu.SemaphoreType.DMA((4,)),
            pltpu.SemaphoreType.DMA((2,)),
        ],
        compiler_params=params(28),
        name="bias",
    )(pinned(pair), pinned(jnp.transpose(w_bias)), pinned(residue_mask.reshape(cols, 1, tile_cols)))
    query_other = sent(query, "cols", lambda c: c ^ half_cols)
    bias_local, kv_first, kv_last, query_other = lax.optimization_barrier(
        (bias_local, kv_first, kv_last, query_other)
    )
    groups = [list(range(half_cols)), list(range(half_cols, cols))]
    bias_heads = lax.all_to_all(bias_local, "cols", 0, 0, axis_index_groups=groups, tiled=True)

    both = jnp.stack([kv_first, kv_last])
    near = [both]
    for s in range(1, shifts):
        around = lambda r: (r & half_rows) | ((r + 2 * s) & (half_rows - 1))
        near.append(sent(both, "rows", around))
    near = jnp.stack(near)
    kv_all = jnp.stack([near, sent(near, "rows", lambda r: r ^ 1)])

    kept, partial, single_near, factors_near, pairout_near, up_near, down_near, out_near = pl.pallas_call(
        attend_kernel,
        out_shape=(
            jax.ShapeDtypeStruct((width + 8, tile_rows), f32),
            jax.ShapeDtypeStruct((width + 16, tile_rows), bf16),
            jax.ShapeDtypeStruct(single.shape, bf16),
            jax.ShapeDtypeStruct(w_factors.shape, bf16),
            jax.ShapeDtypeStruct(w_pairout.shape, bf16),
            jax.ShapeDtypeStruct(w_up.shape, bf16),
            jax.ShapeDtypeStruct(w_down.shape, bf16),
            jax.ShapeDtypeStruct(w_out.shape, bf16),
        ),
        in_specs=[in_vmem] * 4 + [in_hbm] * 6,
        scratch_shapes=[
            pltpu.VMEM((half_cols, tile_rows, tile_cols), f32),
            pltpu.SemaphoreType.DMA((6,)),
        ],
        compiler_params=params(),
        name="attend",
    )(
        query,
        query_other,
        bias_heads,
        kv_all,
        pinned(single),
        pinned(w_factors),
        pinned(w_pairout),
        pinned(w_up),
        pinned(w_down),
        pinned(w_out),
    )
    received = sent(partial, "cols", lambda c: c ^ half_cols)
    mixed = pl.pallas_call(
        join_kernel,
        out_shape=jax.ShapeDtypeStruct((cols, width, tile_rows), bf16),
        compiler_params=params(),
        name="join",
    )(kept, received)
    mixed_all = lax.all_to_all(mixed, "cols", 0, 0, tiled=True).reshape(single_width, tile_rows)

    single_out, factors = pl.pallas_call(
        factor_kernel,
        out_shape=(
            jax.ShapeDtypeStruct(single.shape, bf16),
            jax.ShapeDtypeStruct((tile_rows, w_factors.shape[1]), bf16),
        ),
        compiler_params=params(),
        name="factor",
    )(mixed_all, out_near, single_near, factors_near)

    targets = [nearest_rows(row, rows) for row in range(rows)]
    right_factors = sent(factors, both_axes, lambda r, c: (targets[r][c], r))

    block_rows = 32
    pair_block = pl.BlockSpec((block_rows, tile_cols, pair_width), lambda i: (i, 0, 0))
    updated = pl.pallas_call(
        update_kernel,
        grid=(tile_rows // block_rows,),
        in_specs=[in_vmem] * 6,
        out_specs=pair_block,
        out_shape=jax.ShapeDtypeStruct(pair.shape, bf16),
        scratch_shapes=[
            pltpu.VMEM((tile_rows, 1, pair_width), bf16),
            pltpu.VMEM((tile_rows, 1, pair_width), bf16),
            pltpu.VMEM((tile_cols, pair_width), bf16),
        ],
        compiler_params=params(20),
        name="update",
    )(pair, factors, right_factors, pairout_near, up_near, down_near)
    return (single_out, updated)


def solution(mesh):
    return jax.shard_map(
        per_device,
        mesh=mesh,
        in_specs=(
            P("rows", None),
            P("rows", "cols", None),
            P(),
            P(),
            P(None, None, "cols"),
            P(),
            P(),
            P(),
            P(),
            P(),
        ),
        out_specs=(P("rows", None), P("rows", "cols", None)),
        check_vma=False,
    )
```
